32 devices in a mesh: groups: 2 (over x), date: 16 (over z, y, core).
Axes of the slice: x: 2, y: 2, z: 4, core: 2. Of those that a mesh axis runs over, the one named last changes fastest.
Arguments:
- images: float32 [32, 2, 64, 2560], P(('groups', 'date')), parts along dimension 0, may hold values from -16 to 16
- height_phase: float32 [128, 2560], P(('groups', 'date')), parts along dimension 0, may hold values from -4 to 4
- baseline: float32 [32], P('groups'), parts along dimension 0, may hold values from -0.6 to 0.6
- pair_list: int32 [32, 2], replicated, may hold values from 0 to 15, as said below
- pair_owner: int32 [32, 1], replicated, may hold values from 0 to 15; in each aligned block of 32 rows (0 to 31, 32 to 63, ...) at most 4 rows name the same one
Outputs:
- interferogram: float32 [128, 2, 16, 128], P(('groups', 'date')), parts along dimension 0
- coherence: float32 [128, 16, 128], P(('groups', 'date')), parts along dimension 0
The draws below stay inside these ranges and needn't reach their ends.
There are 2 independent parts, one for each index of `groups`. The reference program is written for one: setup_inputs(seed, part) draws one part's arguments, and reference() takes and returns one part's arrays. A program takes and returns all parts, laid end to end along the dimension named above; an argument that names none is the same for every part. Nothing has to cross between parts.
Inputs may be any that keep to these rules, and one draw needn't show every extreme that they name: `pair_list`: each row is (r, s) with r < s <= r + 4; some pair has s = r + 4. `pair_owner`: every index owns at least one pair and at most 4 pairs; some index owns exactly 4.
All inputs are finite; a program needn't handle non-finite values.
Results may differ from the reference program's by a relative error of at most 0.00007.
Values sent between devices are 32-bit elements; how exact they have to be, the bound alone decides.
A program may use at most 128 MiB of HBM per device.

```python
import math
import jax
import jax.numpy as jnp
import numpy as np
from jax import lax

LOOK_ROWS = 4
LOOK_COLS = 20
BAND = 4
CAP = 4
COLS = 2560
DATES = 16
PAIRS = 32
ROWS = 64
N_DATE = 16


def draw_images(key, part):
    common = jax.random.normal(jax.random.fold_in(key, 101), (2, ROWS, COLS), jnp.float32)
    noise = jax.random.normal(jax.random.fold_in(key, 102), (DATES, 2, ROWS, COLS), jnp.float32)
    spread = math.log(10.0) / 4.0
    low_rho = 0.3
    high_rho = 0.95
    row_scale = jnp.exp(jax.random.uniform(jax.random.fold_in(key, 105), (ROWS,), jnp.float32, -spread, spread))
    col_scale = jnp.exp(jax.random.uniform(jax.random.fold_in(key, 106), (COLS,), jnp.float32, -spread, spread))
    amplitude = row_scale[:, None] * col_scale[None, :]
    rho_value = jax.random.uniform(jax.random.fold_in(key, 107), (DATES,), jnp.float32, low_rho, high_rho)
    angle_value = jax.random.uniform(jax.random.fold_in(key, 108), (DATES,), jnp.float32, -math.pi, math.pi)
    cosine = jnp.cos(angle_value)[:, None, None]
    sine_part = jnp.sin(angle_value)[:, None, None]
    common_real = cosine * common[0][None] - sine_part * common[1][None]
    common_imag = sine_part * common[0][None] + cosine * common[1][None]
    rest = jnp.sqrt(1.0 - rho_value * rho_value)[:, None, None]
    rho_wide = rho_value[:, None, None]
    real_part = amplitude[None] * (rho_wide * common_real + rest * noise[:, 0])
    imag_part = amplitude[None] * (rho_wide * common_imag + rest * noise[:, 1])
    return jnp.clip(jnp.stack([real_part, imag_part], axis=1), -16.0, 16.0).astype(jnp.float32)


def draw_pair_list(key, part):
    first_date = jax.random.randint(jax.random.fold_in(key, 201), (PAIRS,), 0, DATES - BAND, jnp.int32)
    distance = jax.random.randint(jax.random.fold_in(key, 202), (PAIRS,), 1, BAND + 1, jnp.int32)
    position = jnp.arange(PAIRS, dtype=jnp.int32)
    distance = jnp.where(position == 0, BAND, distance)
    return jnp.stack([first_date, first_date + distance], axis=1).astype(jnp.int32)


def shard_levels(own_key, extent, cuts, smallest, largest):
    factor_of = 1.0
    for axis_at, parts in cuts:
        draws = jax.random.uniform(jax.random.fold_in(jax.random.fold_in(own_key, 6), axis_at), (parts,), jnp.float32, smallest / len(cuts), largest / len(cuts))
        factor_of = factor_of * jnp.repeat(jnp.exp(draws), extent[axis_at] // parts).reshape((-1,) + (1,) * (len(extent) - 1 - axis_at))
    return factor_of


def shared_out(own_key, own, number, rows, amount, top, limit, slope):
    sequence = jax.random.permutation(own_key, amount)
    crowded, ordinary = shares(amount, rows * top, limit, slope, True), shares(amount, rows * top, limit, slope, False)
    places = jnp.arange(amount)

    def named(lengths, rotation):
        used = int((lengths > 0).sum())
        fixed = max(1, used // 4)
        passed = fixed + (places - fixed + rotation * (used - fixed)) % max(1, amount - fixed)
        return jnp.zeros((amount,), jnp.int32).at[sequence[jnp.where(places < fixed, places, passed)]].set(jnp.asarray(lengths, jnp.int32))

    lengths = jnp.where(number % 4 == 0, named(crowded, number // 4), named(ordinary, number - number // 4 - 1))
    mixed = jax.random.permutation(jax.random.fold_in(own, 3), amount)
    giver, sink = mixed[0:amount // 2 * 2:2], mixed[1:amount // 2 * 2:2]
    slack = jnp.minimum(lengths[giver] - 1, limit - lengths[sink]) // 2
    slack = jnp.where((giver == sequence[0]) | (sink == sequence[0]) | (lengths[sink] == 0), 0, jnp.maximum(slack, 0))
    passed = jax.random.randint(jax.random.fold_in(own, 4), (amount // 2,), 0, 1 << 20) % (slack + 1)
    lengths = lengths.at[giver].add(-passed).at[sink].add(passed)
    labels = jnp.searchsorted(jnp.cumsum(lengths), jnp.arange(rows * top), side="right").astype(jnp.int32)
    grid = labels.reshape(top, rows).T
    grid = grid[jax.random.permutation(jax.random.fold_in(own, 1), rows)]
    rotation = jax.random.randint(jax.random.fold_in(own, 2), (rows, 1), 0, top)
    return jnp.take_along_axis(grid, (jnp.arange(top)[None, :] + rotation) % top, axis=1)


def shares(number_of, total, bound, skew, full):
    weights = [(1 << 20) // math.isqrt(standing ** skew) + 1 for standing in range(1, number_of + 1)]
    largest = bound if full else min(bound, max(-(-total // number_of), total * weights[0] // sum(weights)))
    least = 1 if total - largest >= number_of - 1 else 0
    counts, spare = [largest] + [least] * (number_of - 1), total - largest - least * (number_of - 1)
    while spare > 0:
        free = [i for i in range(1, number_of) if counts[i] < largest] or [i for i in range(1, number_of) if counts[i] < bound]
        mass, remaining = sum([weights[i] for i in free]), spare
        for i in free:
            extra = min(bound - counts[i], max(1, remaining * weights[i] // mass), spare)
            counts[i] = counts[i] + extra
            spare = spare - extra
    return np.array(counts)


def scatter_about(rng, extent, scale, limit, pieces=(), held_as=jnp.bfloat16):
    values = scale * jax.random.normal(rng, extent, jnp.float32)
    if pieces:
        values = values * shard_levels(rng, extent, pieces, -0.22, 0.18)
    return jnp.clip(values, -limit, limit).astype(held_as)


def setup_inputs(seed: int = 0, part: int = 0) -> dict:
    splits = jax.random.split(jax.random.key(seed), 6)
    part_splits = jax.random.split(jax.random.fold_in(splits[5], part), 6)
    images = draw_images(jax.random.fold_in(jax.random.fold_in(splits[5], part), 71), part)
    height_phase = scatter_about(part_splits[1], (ROWS, COLS), 1.0, 4.0, ((0, 16),), jnp.float32)
    baseline = jnp.clip(jax.random.uniform(part_splits[2], (DATES,), jnp.float32, -0.6, 0.6), -0.6, 0.6)
    pair_list = draw_pair_list(jax.random.fold_in(splits[5], 71), part)
    pair_owner_keys = jax.random.split(jax.random.fold_in(splits[4], 1), PAIRS // PAIRS)
    pair_owner_turns = jax.random.permutation(jax.random.fold_in(splits[4], 3), PAIRS // PAIRS)
    pair_owner = jax.vmap(lambda own, number: shared_out(jax.random.fold_in(splits[4], 2), own, number, PAIRS, N_DATE, 1, CAP, 2))(pair_owner_keys, pair_owner_turns).reshape((PAIRS, 1))
    return {"images": images, "height_phase": height_phase, "baseline": baseline, "pair_list": pair_list, "pair_owner": pair_owner}


EPSILON = 1e-06

def multilook(values):
    values_shape = values.shape
    grouped = values.reshape(values_shape[:-2] + (values_shape[-2] // LOOK_ROWS, LOOK_ROWS, values_shape[-1] // LOOK_COLS, LOOK_COLS))
    return lax.optimization_barrier(jnp.mean(grouped, axis=(-3, -1)))

def flatten_phase(images, factors, height_phase):
    phase_angle = factors[:, None, None] * height_phase[None]
    cosine = jnp.cos(phase_angle)
    sine_part = jnp.sin(phase_angle)
    real_part = images[:, 0] * cosine - images[:, 1] * sine_part
    imag_part = images[:, 0] * sine_part + images[:, 1] * cosine
    return (real_part, imag_part)

def slot_of(pair_owner):
    owners = pair_owner[:, 0]
    position = jnp.arange(owners.shape[0], dtype=jnp.int32)
    earlier = (owners[:, None] == owners[None, :]) & (position[:, None] > position[None, :])
    return (owners * CAP + lax.optimization_barrier(jnp.sum(earlier.astype(jnp.int32), axis=1))).astype(jnp.int32)

def reference(images, height_phase, baseline, pair_list, pair_owner):
    real_part, imag_part = flatten_phase(images, baseline, height_phase)
    power_map = multilook(real_part * real_part + imag_part * imag_part)

    def one_pair(pair_row):
        first_date = pair_row[0]
        second_date = pair_row[1]
        first_real = real_part[first_date]
        first_imag = imag_part[first_date]
        second_real = real_part[second_date]
        second_imag = imag_part[second_date]
        look_real = multilook(first_real * second_real + first_imag * second_imag)
        look_imag = multilook(first_imag * second_real - first_real * second_imag)
        denominator = jnp.sqrt((power_map[first_date] + EPSILON) * (power_map[second_date] + EPSILON))
        coherence = jnp.sqrt(look_real * look_real + look_imag * look_imag) / denominator
        return jnp.stack([look_real, look_imag, coherence])
    results = lax.map(one_pair, pair_list)
    slot_index = slot_of(pair_owner)
    filled = jnp.zeros((CAP * N_DATE,) + results.shape[1:], jnp.float32).at[slot_index].set(results)
    return (filled[:, :2], filled[:, 2])
```

```python
import functools
import math

import jax
import jax.numpy as jnp
from jax import lax
from jax.experimental import pallas as pl
from jax.experimental.pallas import tpu as pltpu
from jax.sharding import PartitionSpec as P

LOOK_ROWS = 4
LOOK_COLS = 20
CAP = 4
BAND = 4
EPSILON = 1e-06
LANES = 128
TILE = 8
HALVES = 2
WIDE = 2
QUANTITIES = 2 + 2 * BAND
UNIT = QUANTITIES * TILE
PIECES = 3
DEPTH = 256
AHEAD = 3
FIRST = 2
START = 6
LAG = 5


def split(values, parts):
    pieces = []
    for _ in range(parts):
        piece = values.astype(jnp.bfloat16)
        pieces.append(piece)
        values = values - piece.astype(jnp.float32)
    return pieces


def cos_sin(angle):
    square = angle * angle
    sine = jnp.full_like(angle, -1.0 / math.factorial(15))
    for term in range(6, -1, -1):
        sine = sine * square + (-1.0) ** term / math.factorial(2 * term + 1)
    cosine = jnp.full_like(angle, 1.0 / math.factorial(16))
    for term in range(7, -1, -1):
        cosine = cosine * square + (-1.0) ** term / math.factorial(2 * term)
    return cosine, sine * angle


def kernel(
    devices, phases, images, height, baseline_in, pair_list_in, pair_owner_in, looks_out, coherence_out,
    window, heights, box, sums, picks, stack, chosen, outbox, inbox, baseline, pair_list, pair_owner,
    far, small_sem, plane_send, relay_send, plane_recv, relay_recv, height_send, height_recv, out_send, out_recv,
):
    me = lax.axis_index("date")
    planes = devices // BAND
    plane = lax.div(me, BAND)
    spot = lax.rem(me, BAND)
    tiles = phases // HALVES
    column_tiles = images.shape[2]
    columns = column_tiles * LANES
    part_columns = columns // HALVES
    steps = part_columns // (LANES * WIDE)
    chunks = phases * steps
    side = BAND * TILE
    dates = 2 * BAND
    part_lanes = LANES // HALVES
    look_rows = TILE // LOOK_ROWS
    below, above = plane > 0, plane < planes - 1

    barrier = pltpu.get_barrier_semaphore()

    def hello(to):
        pl.semaphore_signal(barrier, inc=1, device_id={"date": to})

    for step in range(1, BAND):
        hello(plane * BAND + (spot ^ step))

    @pl.when(below)
    def _():
        hello(me - BAND)

    @pl.when(above)
    def _():
        hello(me + BAND)

    reader = lax.div(me, planes)
    own_height = lax.rem(me, planes)

    def small_copies():
        return [
            pltpu.make_async_copy(source, to, small_sem.at[at])
            for at, (source, to) in enumerate(
                ((baseline_in, baseline), (pair_list_in, pair_list), (pair_owner_in, pair_owner))
            )
        ]

    def height_copy(to_plane):
        return pltpu.make_async_remote_copy(
            src_ref=height,
            dst_ref=heights.at[own_height],
            send_sem=height_send.at[to_plane],
            recv_sem=height_recv.at[own_height],
            device_id={"date": to_plane * BAND + reader},
        )

    def height_own():
        return pltpu.make_async_copy(height, heights.at[own_height], height_recv.at[own_height])

    def height_arrival(source):
        return pltpu.make_async_remote_copy(
            src_ref=height,
            dst_ref=heights.at[source],
            send_sem=height_send.at[0],
            recv_sem=height_recv.at[source],
            device_id={"date": me},
        )

    def lines(quarter, upper, chunk):
        phase = lax.div(chunk, steps)
        tile = (quarter * 2 + upper) * tiles + lax.div(phase, HALVES)
        column = lax.rem(phase, HALVES) * (steps * WIDE) + lax.rem(chunk, steps) * WIDE
        return images.at[:, tile, pl.ds(column, WIDE)]

    def place(upper, chunk, slot, size=TILE):
        return window.at[upper, chunk, :, :, pl.ds(pl.multiple_of(slot * TILE, TILE), size), :]

    def own_slot(upper, which):
        return (1 - upper) * BAND + which

    def plane_copy(step, upper, chunk):
        to = spot ^ step
        return pltpu.make_async_remote_copy(
            src_ref=lines(to, upper, chunk),
            dst_ref=place(upper, chunk, own_slot(upper, spot)),
            send_sem=plane_send.at[upper, chunk],
            recv_sem=plane_recv.at[upper, chunk, spot],
            device_id={"date": plane * BAND + to},
        )

    def plane_arrival(step, upper, chunk):
        source = spot ^ step
        return pltpu.make_async_remote_copy(
            src_ref=lines(source, upper, chunk),
            dst_ref=place(upper, chunk, own_slot(upper, source)),
            send_sem=plane_send.at[upper, chunk],
            recv_sem=plane_recv.at[upper, chunk, source],
            device_id={"date": plane * BAND + source},
        )

    def own_copy(upper, chunk):
        return pltpu.make_async_copy(
            lines(spot, upper, chunk),
            place(upper, chunk, own_slot(upper, spot)),
            plane_recv.at[upper, chunk, spot],
        )

    relays = (above, below)
    gets_relays = (below, above)

    def relay_copy(upper, chunk, which, source):
        return pltpu.make_async_remote_copy(
            src_ref=source,
            dst_ref=place(upper, chunk, upper * BAND + which),
            send_sem=relay_send.at[upper, chunk],
            recv_sem=relay_recv.at[upper, chunk],
            device_id={"date": me + BAND * (1 - 2 * upper)},
        )

    def relay_all(upper, chunk):
        return pltpu.make_async_remote_copy(
            src_ref=place(upper, chunk, (1 - upper) * BAND, side),
            dst_ref=place(upper, chunk, upper * BAND, side),
            send_sem=relay_send.at[upper, chunk],
            recv_sem=relay_recv.at[upper, chunk],
            device_id={"date": me},
        )

    def plane_all(upper, chunk):
        return pltpu.make_async_remote_copy(
            src_ref=place(upper, chunk, 0, side - TILE),
            dst_ref=place(upper, chunk, 0, side - TILE),
            send_sem=plane_send.at[upper, chunk],
            recv_sem=relay_recv.at[upper, chunk],
            device_id={"date": me},
        )

    def own_relays(chunk):
        for upper in range(2):
            @pl.when(relays[upper])
            def _():
                relay_copy(upper, chunk, spot, lines(spot, upper, chunk)).start()

    for copy in small_copies():
        copy.start()
    pl.semaphore_wait(barrier, BAND - 1 + jnp.where(below, 1, 0) + jnp.where(above, 1, 0))

    def rows_out(chunk):
        for step in (2, 3, 1):
            for upper in range(2):
                plane_copy(step, upper, chunk).start()
        for upper in range(2):
            own_copy(upper, chunk).start()

    @pl.loop(0, FIRST)
    def _(chunk):
        rows_out(chunk)

    @pl.loop(0, AHEAD)
    def _(chunk):
        own_relays(chunk)

    for turn in range(planes - 1):
        @pl.when(below)
        def _():
            pl.semaphore_signal(far.at[turn], inc=1, device_id={"date": me - BAND})

        @pl.when(above)
        def _():
            pl.semaphore_signal(far.at[turn], inc=1, device_id={"date": me + BAND})

        pl.semaphore_wait(far.at[turn], jnp.where(below, 1, 0) + jnp.where(above, 1, 0))

    @pl.loop(0, planes)
    def _(to_plane):
        @pl.when(to_plane * BAND + reader != me)
        def _():
            height_copy(to_plane).start()

        @pl.when(to_plane * BAND + reader == me)
        def _():
            height_own().start()

    @pl.loop(FIRST, chunks)
    def _(chunk):
        rows_out(chunk)

    for upper in range(2):
        @pl.when(jnp.logical_not(gets_relays[upper]))
        def _():
            @pl.loop(0, chunks)
            def _(chunk):
                window[upper, chunk, :, :, upper * side:(upper + 1) * side, :] = jnp.zeros(
                    (2, WIDE, side, LANES), jnp.float32
                )

    @pl.loop(0, steps * WIDE)
    def _(block):
        shape = (look_rows * LANES, LANES)
        line = lax.broadcasted_iota(jnp.int32, shape, 0)
        position = block * LANES + (line & (LANES - 1))
        target = lax.broadcasted_iota(jnp.int32, shape, 1) - jnp.where(line >= LANES, part_lanes, 0)
        target = target * LOOK_COLS
        box[pl.ds(pl.multiple_of(block * look_rows * LANES, look_rows * LANES), look_rows * LANES), :] = jnp.where(
            (position >= target) & (position < target + LOOK_COLS), 1.0, 0.0
        ).astype(jnp.bfloat16)

    sums[...] = jnp.zeros_like(sums)
    stack[...] = jnp.zeros_like(stack)

    for copy in small_copies():
        copy.wait()

    lane = lax.broadcasted_iota(jnp.int32, (dates, devices), 1)
    date = lax.broadcasted_iota(jnp.int32, (dates, devices), 0)
    scales = []
    for upper in range(2):
        chosen_date = lane == date + (plane - 1 + upper) * BAND
        scales.append(
            jnp.sum(jnp.where(chosen_date, baseline[...], 0.0), axis=1, keepdims=True)
        )

    owner = pair_owner[...]
    pairs = owner.shape[1]
    down = lax.broadcasted_iota(jnp.int32, (pairs, pairs), 0)
    across = lax.broadcasted_iota(jnp.int32, (pairs, pairs), 1)
    owner_column = jnp.sum(jnp.where(down == across, owner, 0), axis=1, keepdims=True)
    earlier = (owner_column == owner) & (down < across)
    slot_of = owner * CAP + jnp.sum(jnp.where(earlier, 1, 0), axis=0, keepdims=True)
    first, second = pair_list[0:1, :], pair_list[1:2, :]
    distance = second - first
    first_here = lax.div(first, BAND) == plane
    second_here = lax.div(second, BAND) == plane
    first_at = lax.rem(first, BAND)
    second_at = lax.rem(second, BAND)
    others = (QUANTITIES - 1) * TILE
    places = (
        (first_here, first_at + distance * TILE),
        (first_here, first_at + (BAND + distance) * TILE),
        (second_here, second_at + distance * TILE + BAND),
        (second_here, second_at + (BAND + distance) * TILE + BAND),
        (first_here, first_at),
        (second_here, jnp.where(first_here, first_at + BAND, others + first_at)),
        (first_here, jnp.where(second_here, second_at, others + second_at + BAND)),
        (second_here, second_at + BAND),
    )
    total = devices * len(places) * CAP
    line = lax.broadcasted_iota(jnp.int32, (total, pairs), 0)
    part = (line & (len(places) * CAP - 1)) - (line & (CAP - 1))
    taken = lax.div(line, len(places)) - lax.div(line & (len(places) * CAP - 1), len(places)) + (line & (CAP - 1)) == slot_of
    listed = jnp.full((total, pairs), -1, jnp.int32)
    for at, (valid, value) in enumerate(places):
        listed = jnp.where(taken & valid & (part == at * CAP), value, listed)
    listed = jnp.max(listed.astype(jnp.float32), axis=1, keepdims=True)
    depth = lax.broadcasted_iota(jnp.int32, (total, DEPTH), 1).astype(jnp.float32)
    hit = (depth == listed)
    for piece in range(1, PIECES):
        hit = hit | (depth == listed + piece * UNIT)
    picks[...] = jnp.where(hit & (listed >= 0.0), 1.0, 0.0).astype(jnp.bfloat16)

    def forward(chunk):
        @pl.when(chunk + AHEAD < chunks)
        def _():
            own_relays(chunk + AHEAD)

        for step in (1, 2, 3):
            for upper in range(2):
                plane_arrival(step, upper, chunk).wait_recv()

                @pl.when(relays[upper])
                def _():
                    which = spot ^ step
                    relay_copy(
                        upper, chunk, which, place(upper, chunk, own_slot(upper, which))
                    ).start()

    own_rows = lax.broadcasted_iota(jnp.int32, (dates, LANES), 0) < BAND

    def compute(chunk):
        for upper in range(2):
            own_copy(upper, chunk).wait()

            @pl.when(gets_relays[upper])
            def _():
                relay_all(upper, chunk).wait_recv()

        phase = lax.div(chunk, steps)
        tile = lax.div(phase, HALVES)
        step = lax.rem(chunk, steps)

        @pl.loop(0, WIDE)
        def _(block):
            column = pl.multiple_of(
                (lax.rem(phase, HALVES) * (steps * WIDE) + step * WIDE + block) * LANES, LANES
            )
            totals = []
            for look_row in range(look_rows):
                found = [None] * QUANTITIES

                def add(at, value):
                    found[at] = value if found[at] is None else found[at] + value

                for row in range(LOOK_ROWS):
                    flat = []
                    for upper in range(2):
                        source = (upper * tiles + tile) * look_rows + look_row
                        level = heights[source, row:row + 1, pl.ds(column, LANES)]
                        cosine, sine = cos_sin(scales[upper] * level)
                        at = pl.ds(look_row * LOOK_ROWS + row, dates, stride=TILE)
                        real = window[upper, chunk, 0, block, at, :]
                        imag = window[upper, chunk, 1, block, at, :]
                        flat.append((real * cosine - imag * sine, real * sine + imag * cosine))
                    own_real, own_imag = (jnp.where(own_rows, u, l) for l, u in zip(*flat))
                    add(0, own_real * own_real + own_imag * own_imag)
                    rest_real, rest_imag = (jnp.where(own_rows, l, u) for l, u in zip(*flat))
                    add(QUANTITIES - 1, rest_real * rest_real + rest_imag * rest_imag)
                    for distance in range(1, BAND + 1):
                        other_real, other_imag = (
                            jnp.where(
                                own_rows, pltpu.roll(u, dates - distance, 0), pltpu.roll(l, distance, 0)
                            )
                            for l, u in zip(*flat)
                        )
                        add(distance, own_real * other_real + own_imag * other_imag)
                        add(BAND + distance, own_imag * other_real - own_real * other_imag)
                totals.append(jnp.concatenate(found, axis=0))
            weights = box[
                pl.ds(pl.multiple_of((step * WIDE + block) * look_rows * LANES, LANES), look_rows * LANES), :
            ]
            summed = sums[phase]
            for piece in split(jnp.concatenate(totals, axis=1), 2):
                summed = summed + jnp.dot(piece, weights, preferred_element_type=jnp.float32)
            sums[phase] = summed

    def done(step):
        return jnp.maximum(0, jnp.minimum(2 * (step - START), step - LAG))

    @pl.loop(0, chunks + LAG)
    def _(step):
        @pl.when(step < chunks)
        def _():
            forward(step)

        @pl.when(step == START)
        def _():
            @pl.loop(0, planes)
            def _(source):
                height_arrival(source).wait_recv()

        @pl.loop(done(step), done(step + 1))
        def _(chunk):
            compute(chunk)

    line = lax.broadcasted_iota(jnp.int32, (UNIT, LANES), 0)
    turned = (line >= (1 + BAND) * TILE) & (line < (1 + 2 * BAND) * TILE) & ((line & BAND) == BAND)
    scale = jnp.where(turned, -1.0, 1.0) * (1.0 / (LOOK_ROWS * LOOK_COLS))
    size = len(places) * CAP
    for tile in range(tiles):
        for half in range(HALVES):
            for at, piece in enumerate(split(sums[tile * HALVES + half] * scale, PIECES)):
                stack[at * UNIT:(at + 1) * UNIT, half * LANES:(half + 1) * LANES] = piece
        chosen[...] = jnp.dot(picks[...], stack[...], preferred_element_type=jnp.float32)

        @pl.loop(0, devices // BAND)
        def _(some):
            for one in range(BAND):
                which = some * BAND + one
                for half in range(HALVES):
                    near, far_side, first_power, second_power = (
                        chosen[
                            pl.ds(pl.multiple_of(which * size + at * TILE, TILE), TILE),
                            half * LANES:(half + 1) * LANES,
                        ]
                        for at in range(4)
                    )
                    squares = [v * v for v in (near, far_side)]
                    squares = [v + pltpu.roll(v, CAP, 0) for v in squares]
                    level = jnp.sqrt(jnp.where(own_rows, squares[0], squares[1]))
                    ratio = level / jnp.sqrt((first_power + EPSILON) * (second_power + EPSILON))
                    for at, value in enumerate((near, far_side, ratio)):
                        outbox[which, (tile * HALVES + half) * 3 + at] = value

    def peer(step):
        return lax.rem(me + step, devices)

    def out_copy(to):
        return pltpu.make_async_remote_copy(
            src_ref=outbox.at[to],
            dst_ref=inbox.at[me],
            send_sem=out_send.at[to],
            recv_sem=out_recv.at[me],
            device_id={"date": to},
        )

    def out_arrival(source):
        return pltpu.make_async_remote_copy(
            src_ref=outbox.at[source],
            dst_ref=inbox.at[source],
            send_sem=out_send.at[source],
            recv_sem=out_recv.at[source],
            device_id={"date": source},
        )

    @pl.loop(1, devices)
    def _(step):
        out_copy(peer(step)).start()

    inbox[me] = outbox[me]

    @pl.loop(0, planes)
    def _(to_plane):
        @pl.when(to_plane * BAND + reader != me)
        def _():
            height_copy(to_plane).wait_send()

    @pl.loop(0, chunks)
    def _(chunk):
        for upper in range(2):
            plane_all(upper, chunk).wait_send()

            @pl.when(relays[upper])
            def _():
                relay_all(upper, chunk).wait_send()

    @pl.loop(1, devices)
    def _(step):
        out_arrival(peer(step)).wait_recv()

    looks = coherence_out.shape[0] // CAP
    left = lax.broadcasted_iota(jnp.int32, (TILE, LANES), 1) < part_lanes
    for quarter in range(BAND):
        for tile in range(tiles):
            for part in range(3):
                sides = []
                for half in range(HALVES):
                    at = (tile * HALVES + half) * 3 + part
                    value = inbox[quarter, at]
                    for other in range(1, planes):
                        value = value + inbox[other * BAND + quarter, at]
                    sides.append(value)
                here, there = sides
                values = (
                    jnp.where(left, here, pltpu.roll(there, part_lanes, 1)),
                    jnp.where(left, pltpu.roll(here, part_lanes, 1), there),
                )
                for look_row, value in enumerate(values):
                    for c in range(2):
                        upper = 1 - part if part < 2 else 1 - c
                        at = ((quarter * 2 + upper) * tiles + tile) * look_rows + look_row
                        piece = value[c * CAP:(c + 1) * CAP]
                        if part < 2:
                            looks_out[pl.ds(c * looks + at, CAP, stride=2 * looks), :] = piece
                        else:
                            coherence_out[pl.ds(at, CAP, stride=looks), :] = piece

    @pl.loop(1, devices)
    def _(step):
        out_copy(peer(step)).wait_send()


def body(images, height_phase, baseline, pair_list, pair_owner):
    devices = lax.axis_size("date")
    rows, columns = images.shape[2:]
    lanes = columns // LOOK_COLS
    looks = rows // LOOK_ROWS
    planes = devices // BAND
    tiles = rows // (2 * BAND * TILE)
    phases = tiles * HALVES
    chunks = phases * (columns // (HALVES * LANES * WIDE))
    dates = 2 * BAND
    pairs = pair_list.shape[0]
    assert lanes == LANES and rows == LOOK_ROWS * devices and TILE == 2 * LOOK_ROWS and HALVES == 2
    assert rows % (2 * BAND * TILE) == 0 and columns % (HALVES * LANES * WIDE) == 0
    assert PIECES * UNIT <= DEPTH
    vmem = pl.BlockSpec(memory_space=pltpu.VMEM)
    hbm = pl.BlockSpec(memory_space=pltpu.HBM)
    dma = pltpu.SemaphoreType.DMA
    tiled = images[0].reshape(2, rows // TILE, TILE, columns // LANES, LANES).transpose(0, 1, 3, 2, 4)
    inputs = [
        pltpu.with_memory_space_constraint(v, pltpu.HBM)
        for v in (tiled, height_phase, baseline[None], pair_list.T, pair_owner.T)
    ]
    scratch = [
        pltpu.VMEM((2, chunks, 2, WIDE, dates * TILE, LANES), jnp.float32),
        pltpu.VMEM((planes, LOOK_ROWS, columns), jnp.float32),
        pltpu.VMEM((2 * columns // HALVES, lanes), jnp.bfloat16),
        pltpu.VMEM((phases, UNIT, lanes), jnp.float32),
        pltpu.VMEM((devices * TILE * CAP, DEPTH), jnp.bfloat16),
        pltpu.VMEM((DEPTH, HALVES * lanes), jnp.bfloat16),
        pltpu.VMEM((devices * TILE * CAP, HALVES * lanes), jnp.float32),
        pltpu.VMEM((devices, phases * 3, TILE, lanes), jnp.float32),
        pltpu.VMEM((devices, phases * 3, TILE, lanes), jnp.float32),
        pltpu.VMEM((1, devices), jnp.float32),
        pltpu.VMEM((2, pairs), jnp.int32),
        pltpu.VMEM((1, pairs), jnp.int32),
    ]
    size = sum(math.prod(s.shape) * jnp.dtype(s.dtype).itemsize for s in scratch)
    scratch += [
        pltpu.SemaphoreType.REGULAR((planes - 1,)),
        dma((3,)),
        dma((2, chunks)),
        dma((2, chunks)),
        dma((2, chunks, BAND)),
        dma((2, chunks)),
        dma((planes,)),
        dma((planes,)),
        dma((devices,)),
        dma((devices,)),
    ]
    look, coherence = pl.pallas_call(
        functools.partial(kernel, devices, phases),
        out_shape=(
            jax.ShapeDtypeStruct((CAP * 2 * looks, lanes), jnp.float32),
            jax.ShapeDtypeStruct((CAP * looks, lanes), jnp.float32),
        ),
        in_specs=[hbm] * 5,
        out_specs=(vmem, vmem),
        scratch_shapes=scratch,
        compiler_params=pltpu.CompilerParams(
            collective_id=0, has_side_effects=True, vmem_limit_bytes=size + (6 << 20)
        ),
    )(*inputs)
    return look.reshape(CAP, 2, looks, lanes), coherence.reshape(CAP, looks, lanes)


def solution(mesh):
    in_specs = (
        P(("groups", "date"), None, None, None),
        P(("groups", "date"), None),
        P("groups"),
        P(),
        P(),
    )
    out_specs = (P(("groups", "date"), None, None, None), P(("groups", "date"), None, None))
    return jax.shard_map(body, mesh=mesh, in_specs=in_specs, out_specs=out_specs, check_vma=False)
```

```python
import functools
import math

import jax
import jax.numpy as jnp
from jax import lax
from jax.experimental import pallas as pl
from jax.experimental.pallas import tpu as pltpu
from jax.sharding import PartitionSpec as P

LOOK_ROWS = 4
LOOK_COLS = 20
CAP = 4
BAND = 4
EPSILON = 1e-06
LANES = 128
TILE = 8
HALVES = 2
WIDE = 2
QUANTITIES = 2 + 2 * BAND
LINES = QUANTITIES * TILE
UNIT = LINES - TILE
PARTS = 8
PIECES = 3
DEPTH = 256
AHEAD = 3
FIRST = 2
START = 6
LAG = 5


def split(values, parts):
    pieces = []
    for _ in range(parts):
        piece = values.astype(jnp.bfloat16)
        pieces.append(piece)
        values = values - piece.astype(jnp.float32)
    return pieces


def cos_sin(angle):
    square = angle * angle
    sine = jnp.full_like(angle, -1.0 / math.factorial(15))
    for term in range(6, -1, -1):
        sine = sine * square + (-1.0) ** term / math.factorial(2 * term + 1)
    cosine = jnp.full_like(angle, 1.0 / math.factorial(16))
    for term in range(7, -1, -1):
        cosine = cosine * square + (-1.0) ** term / math.factorial(2 * term)
    return cosine, sine * angle


def kernel(
    devices, phases, images, height, baseline_in, pair_list_in, pair_owner_in, looks_out, coherence_out,
    window, heights, box, sums, picks, stack, chosen, outbox, inbox, baseline, pair_list, pair_owner,
    table, index, staged, plane_inbox, *rest,
):
    early = phases - 1
    units, outboxes = rest[:early], rest[early:2 * early]
    (
        far, small_sem, plane_send, relay_send, plane_recv, relay_recv, height_send, height_recv,
        unit_send, unit_recv, slot_send, slot_recv, out_send, out_recv,
    ) = rest[2 * early:]
    me = lax.axis_index("date")
    planes = devices // BAND
    plane = lax.div(me, BAND)
    spot = lax.rem(me, BAND)
    tiles = phases // HALVES
    column_tiles = images.shape[2]
    columns = column_tiles * LANES
    part_columns = columns // HALVES
    steps = part_columns // (LANES * WIDE)
    chunks = phases * steps
    side = BAND * TILE
    dates = 2 * BAND
    part_lanes = LANES // HALVES
    look_rows = TILE // LOOK_ROWS
    below, above = plane > 0, plane < planes - 1

    barrier = pltpu.get_barrier_semaphore()

    def hello(to):
        pl.semaphore_signal(barrier, inc=1, device_id={"date": to})

    for step in range(1, BAND):
        hello(plane * BAND + (spot ^ step))

    @pl.when(below)
    def _():
        hello(me - BAND)

    @pl.when(above)
    def _():
        hello(me + BAND)

    reader = lax.div(me, planes)
    own_height = lax.rem(me, planes)

    def small_copies():
        return [
            pltpu.make_async_copy(source, to, small_sem.at[at])
            for at, (source, to) in enumerate(
                ((baseline_in, baseline), (pair_list_in, pair_list), (pair_owner_in, pair_owner))
            )
        ]

    def height_copy(to_plane):
        return pltpu.make_async_remote_copy(
            src_ref=height,
            dst_ref=heights.at[own_height],
            send_sem=height_send.at[to_plane],
            recv_sem=height_recv.at[own_height],
            device_id={"date": to_plane * BAND + reader},
        )

    def height_own():
        return pltpu.make_async_copy(height, heights.at[own_height], height_recv.at[own_height])

    def height_arrival(source):
        return pltpu.make_async_remote_copy(
            src_ref=height,
            dst_ref=heights.at[source],
            send_sem=height_send.at[0],
            recv_sem=height_recv.at[source],
            device_id={"date": me},
        )

    def lines(quarter, upper, chunk):
        phase = lax.div(chunk, steps)
        tile = (quarter * 2 + upper) * tiles + lax.div(phase, HALVES)
        column = lax.rem(phase, HALVES) * (steps * WIDE) + lax.rem(chunk, steps) * WIDE
        return images.at[:, tile, pl.ds(column, WIDE)]

    def place(upper, chunk, slot, size=TILE):
        return window.at[upper, chunk, :, :, pl.ds(pl.multiple_of(slot * TILE, TILE), size), :]

    def own_slot(upper, which):
        return (1 - upper) * BAND + which

    def plane_copy(step, upper, chunk):
        to = spot ^ step
        return pltpu.make_async_remote_copy(
            src_ref=lines(to, upper, chunk),
            dst_ref=place(upper, chunk, own_slot(upper, spot)),
            send_sem=plane_send.at[upper, chunk],
            recv_sem=plane_recv.at[upper, chunk, spot],
            device_id={"date": plane * BAND + to},
        )

    def plane_arrival(step, upper, chunk):
        source = spot ^ step
        return pltpu.make_async_remote_copy(
            src_ref=lines(source, upper, chunk),
            dst_ref=place(upper, chunk, own_slot(upper, source)),
            send_sem=plane_send.at[upper, chunk],
            recv_sem=plane_recv.at[upper, chunk, source],
            device_id={"date": plane * BAND + source},
        )

    def own_copy(upper, chunk):
        return pltpu.make_async_copy(
            lines(spot, upper, chunk),
            place(upper, chunk, own_slot(upper, spot)),
            plane_recv.at[upper, chunk, spot],
        )

    relays = (above, below)
    gets_relays = (below, above)

    def relay_copy(upper, chunk, which, source):
        return pltpu.make_async_remote_copy(
            src_ref=source,
            dst_ref=place(upper, chunk, upper * BAND + which),
            send_sem=relay_send.at[upper, chunk],
            recv_sem=relay_recv.at[upper, chunk],
            device_id={"date": me + BAND * (1 - 2 * upper)},
        )

    def relay_all(upper, chunk):
        return pltpu.make_async_remote_copy(
            src_ref=place(upper, chunk, (1 - upper) * BAND, side),
            dst_ref=place(upper, chunk, upper * BAND, side),
            send_sem=relay_send.at[upper, chunk],
            recv_sem=relay_recv.at[upper, chunk],
            device_id={"date": me},
        )

    def plane_all(upper, chunk):
        return pltpu.make_async_remote_copy(
            src_ref=place(upper, chunk, 0, side - TILE),
            dst_ref=place(upper, chunk, 0, side - TILE),
            send_sem=plane_send.at[upper, chunk],
            recv_sem=relay_recv.at[upper, chunk],
            device_id={"date": me},
        )

    def own_relays(chunk):
        for upper in range(2):
            @pl.when(relays[upper])
            def _():
                relay_copy(upper, chunk, spot, lines(spot, upper, chunk)).start()

    for copy in small_copies():
        copy.start()
    pl.semaphore_wait(barrier, BAND - 1 + jnp.where(below, 1, 0) + jnp.where(above, 1, 0))

    def rows_out(chunk):
        for step in (2, 3, 1):
            for upper in range(2):
                plane_copy(step, upper, chunk).start()
        for upper in range(2):
            own_copy(upper, chunk).start()

    @pl.loop(0, FIRST)
    def _(chunk):
        rows_out(chunk)

    @pl.loop(0, AHEAD)
    def _(chunk):
        own_relays(chunk)

    for turn in range(planes - 1):
        @pl.when(below)
        def _():
            pl.semaphore_signal(far.at[turn], inc=1, device_id={"date": me - BAND})

        @pl.when(above)
        def _():
            pl.semaphore_signal(far.at[turn], inc=1, device_id={"date": me + BAND})

        pl.semaphore_wait(far.at[turn], jnp.where(below, 1, 0) + jnp.where(above, 1, 0))

    @pl.loop(0, planes)
    def _(to_plane):
        @pl.when(to_plane * BAND + reader != me)
        def _():
            height_copy(to_plane).start()

        @pl.when(to_plane * BAND + reader == me)
        def _():
            height_own().start()

    @pl.loop(FIRST, chunks)
    def _(chunk):
        rows_out(chunk)

    for upper in range(2):
        @pl.when(jnp.logical_not(gets_relays[upper]))
        def _():
            @pl.loop(0, chunks)
            def _(chunk):
                window[upper, chunk, :, :, upper * side:(upper + 1) * side, :] = jnp.zeros(
                    (2, WIDE, side, LANES), jnp.float32
                )

    @pl.loop(0, steps * WIDE)
    def _(block):
        shape = (look_rows * LANES, LANES)
        line = lax.broadcasted_iota(jnp.int32, shape, 0)
        position = block * LANES + (line & (LANES - 1))
        target = lax.broadcasted_iota(jnp.int32, shape, 1) - jnp.where(line >= LANES, part_lanes, 0)
        target = target * LOOK_COLS
        box[pl.ds(pl.multiple_of(block * look_rows * LANES, look_rows * LANES), look_rows * LANES), :] = jnp.where(
            (position >= target) & (position < target + LOOK_COLS), 1.0, 0.0
        ).astype(jnp.bfloat16)

    sums[...] = jnp.zeros_like(sums)
    stack[...] = jnp.zeros_like(stack)

    for copy in small_copies():
        copy.wait()

    lane = lax.broadcasted_iota(jnp.int32, (dates, devices), 1)
    date = lax.broadcasted_iota(jnp.int32, (dates, devices), 0)
    scales = []
    for upper in range(2):
        chosen_date = lane == date + (plane - 1 + upper) * BAND
        scales.append(
            jnp.sum(jnp.where(chosen_date, baseline[...], 0.0), axis=1, keepdims=True)
        )

    owner = pair_owner[...]
    pairs = owner.shape[1]
    down = lax.broadcasted_iota(jnp.int32, (pairs, pairs), 0)
    across = lax.broadcasted_iota(jnp.int32, (pairs, pairs), 1)
    owner_column = jnp.sum(jnp.where(down == across, owner, 0), axis=1, keepdims=True)
    earlier = (owner_column == owner) & (down < across)
    slot_of = owner * CAP + jnp.sum(jnp.where(earlier, 1, 0), axis=0, keepdims=True)
    first, second = pair_list[0:1, :], pair_list[1:2, :]
    distance = second - first
    first_here = lax.div(first, BAND) == plane
    second_here = lax.div(second, BAND) == plane
    first_at = lax.rem(first, BAND)
    second_at = lax.rem(second, BAND)
    others = (QUANTITIES - 1) * TILE
    places = (
        (first_here, first_at + distance * TILE),
        (first_here, first_at + (BAND + distance) * TILE),
        (second_here, second_at + distance * TILE + BAND),
        (second_here, second_at + (BAND + distance) * TILE + BAND),
        (first_here, first_at),
        (second_here, jnp.where(first_here, first_at + BAND, others + first_at)),
        (first_here, jnp.where(second_here, second_at, others + second_at + BAND)),
        (second_here, second_at + BAND),
    )
    total = devices * len(places) * CAP
    line = lax.broadcasted_iota(jnp.int32, (total, pairs), 0)
    part = (line & (len(places) * CAP - 1)) - (line & (CAP - 1))
    taken = lax.div(line, len(places)) - lax.div(line & (len(places) * CAP - 1), len(places)) + (line & (CAP - 1)) == slot_of
    listed = jnp.full((total, pairs), -1, jnp.int32)
    for at, (valid, value) in enumerate(places):
        listed = jnp.where(taken & valid & (part == at * CAP), value, listed)
    listed = jnp.max(listed.astype(jnp.float32), axis=1, keepdims=True)
    depth = lax.broadcasted_iota(jnp.int32, (total, DEPTH), 1).astype(jnp.float32)
    hit = (depth == listed)
    for piece in range(1, PIECES):
        hit = hit | (depth == listed + piece * LINES)
    picks[...] = jnp.where(hit & (listed >= 0.0), 1.0, 0.0).astype(jnp.bfloat16)

    first_line = lax.div(first, BAND) * UNIT + first_at
    second_line = lax.div(second, BAND) * UNIT + second_at
    lines_of = (
        first_line + distance * TILE,
        first_line + (BAND + distance) * TILE,
        second_line + distance * TILE + BAND,
        second_line + (BAND + distance) * TILE + BAND,
        first_line,
        first_line + BAND,
        second_line,
        second_line + BAND,
    )
    slots = BAND * CAP
    empty = planes * UNIT
    slot = lax.broadcasted_iota(jnp.int32, (slots, pairs), 0) + plane * slots
    taken = slot == slot_of
    table_lane = lax.broadcasted_iota(jnp.int32, (slots, LANES), 1)
    entries = jnp.zeros((slots, LANES), jnp.int32)
    for at, value in enumerate(lines_of):
        listed = empty + jnp.sum(jnp.where(taken, value - empty, 0), axis=1, keepdims=True)
        entries = jnp.where(table_lane == at, listed, entries)
    table[...] = jnp.clip(entries, 0, empty)
    index_copy = pltpu.make_async_copy(table, index, small_sem.at[3])
    index_copy.start()
    for unit in units:
        unit[empty:, :] = jnp.zeros((TILE, LANES), jnp.float32)

    def forward(chunk):
        @pl.when(chunk + AHEAD < chunks)
        def _():
            own_relays(chunk + AHEAD)

        for step in (1, 2, 3):
            for upper in range(2):
                plane_arrival(step, upper, chunk).wait_recv()

                @pl.when(relays[upper])
                def _():
                    which = spot ^ step
                    relay_copy(
                        upper, chunk, which, place(upper, chunk, own_slot(upper, which))
                    ).start()

    own_rows = lax.broadcasted_iota(jnp.int32, (dates, LANES), 0) < BAND

    def compute(chunk):
        for upper in range(2):
            own_copy(upper, chunk).wait()

            @pl.when(gets_relays[upper])
            def _():
                relay_all(upper, chunk).wait_recv()

        phase = lax.div(chunk, steps)
        tile = lax.div(phase, HALVES)
        step = lax.rem(chunk, steps)

        @pl.loop(0, WIDE)
        def _(block):
            column = pl.multiple_of(
                (lax.rem(phase, HALVES) * (steps * WIDE) + step * WIDE + block) * LANES, LANES
            )
            totals = []
            for look_row in range(look_rows):
                found = [None] * QUANTITIES

                def add(at, value):
                    found[at] = value if found[at] is None else found[at] + value

                for row in range(LOOK_ROWS):
                    flat = []
                    for upper in range(2):
                        source = (upper * tiles + tile) * look_rows + look_row
                        level = heights[source, row:row + 1, pl.ds(column, LANES)]
                        cosine, sine = cos_sin(scales[upper] * level)
                        at = pl.ds(look_row * LOOK_ROWS + row, dates, stride=TILE)
                        real = window[upper, chunk, 0, block, at, :]
                        imag = window[upper, chunk, 1, block, at, :]
                        flat.append((real * cosine - imag * sine, real * sine + imag * cosine))
                    own_real, own_imag = (jnp.where(own_rows, u, l) for l, u in zip(*flat))
                    add(0, own_real * own_real + own_imag * own_imag)
                    rest_real, rest_imag = (jnp.where(own_rows, l, u) for l, u in zip(*flat))
                    add(QUANTITIES - 1, rest_real * rest_real + rest_imag * rest_imag)
                    for distance in range(1, BAND + 1):
                        other_real, other_imag = (
                            jnp.where(
                                own_rows, pltpu.roll(u, dates - distance, 0), pltpu.roll(l, distance, 0)
                            )
                            for l, u in zip(*flat)
                        )
                        add(distance, own_real * other_real + own_imag * other_imag)
                        add(BAND + distance, own_imag * other_real - own_real * other_imag)
                totals.append(jnp.concatenate(found, axis=0))
            weights = box[
                pl.ds(pl.multiple_of((step * WIDE + block) * look_rows * LANES, LANES), look_rows * LANES), :
            ]
            summed = sums[phase]
            for piece in split(jnp.concatenate(totals, axis=1), 2):
                summed = summed + jnp.dot(piece, weights, preferred_element_type=jnp.float32)
            sums[phase] = summed

    line = lax.broadcasted_iota(jnp.int32, (LINES, LANES), 0)
    turned = (line >= (1 + BAND) * TILE) & (line < (1 + 2 * BAND) * TILE) & ((line & BAND) == BAND)
    scale = jnp.where(turned, -1.0, 1.0) * (1.0 / (LOOK_ROWS * LOOK_COLS))

    def unit_lines(phase, which):
        return units[phase].at[pl.ds(pl.multiple_of(which * UNIT, TILE), UNIT), :]

    def unit_copy(phase, to_plane):
        return pltpu.make_async_remote_copy(
            src_ref=unit_lines(phase, plane),
            dst_ref=unit_lines(phase, plane),
            send_sem=unit_send.at[phase, to_plane],
            recv_sem=unit_recv.at[phase, plane],
            device_id={"date": to_plane * BAND + spot},
        )

    def unit_arrival(phase, source):
        return pltpu.make_async_remote_copy(
            src_ref=unit_lines(phase, source),
            dst_ref=unit_lines(phase, source),
            send_sem=unit_send.at[phase, source],
            recv_sem=unit_recv.at[phase, source],
            device_id={"date": source * BAND + spot},
        )

    def other_plane(turn):
        return lax.rem(plane + turn, planes)

    def unit_start(phase):
        units[phase][pl.ds(pl.multiple_of(plane * UNIT, TILE), UNIT), :] = sums[phase, :UNIT] * scale[:UNIT]

        @pl.loop(1, planes)
        def _(turn):
            unit_copy(phase, other_plane(turn)).start()

    def ratio_of(near, far_side, first_power, second_power):
        squares = [v * v for v in (near, far_side)]
        squares = [v + pltpu.roll(v, CAP, 0) for v in squares]
        level = jnp.sqrt(jnp.where(own_rows, squares[0], squares[1]))
        return level / jnp.sqrt((first_power + EPSILON) * (second_power + EPSILON))

    def parcel(to):
        return pl.ds(pl.multiple_of(to * 3 * TILE, TILE), 3 * TILE)

    def slot_copy(phase, to):
        return pltpu.make_async_remote_copy(
            src_ref=outboxes[phase].at[parcel(to), :],
            dst_ref=plane_inbox.at[phase, spot],
            send_sem=slot_send.at[phase, to],
            recv_sem=slot_recv.at[phase, spot],
            device_id={"date": plane * BAND + to},
        )

    def slot_arrival(phase, source):
        return pltpu.make_async_remote_copy(
            src_ref=outboxes[phase].at[parcel(source), :],
            dst_ref=plane_inbox.at[phase, source],
            send_sem=slot_send.at[phase, source],
            recv_sem=slot_recv.at[phase, source],
            device_id={"date": plane * BAND + source},
        )

    def choose(phase):
        unit = units[phase]
        for which in range(BAND):
            for at in range(CAP):
                for part in range(PARTS):
                    line = jnp.clip(index[which * CAP + at, part], 0, planes * UNIT)
                    row = (which * 4 + part // 2) * TILE + part % 2 * CAP + at
                    staged[phase, row:row + 1, :] = unit[pl.ds(line, 1), :]
        for which in range(BAND):
            near, far_side, first_power, second_power = (
                staged[phase, (which * 4 + at) * TILE:(which * 4 + at + 1) * TILE, :] for at in range(4)
            )
            ratio = ratio_of(near, far_side, first_power, second_power)
            outboxes[phase][which * 3 * TILE:(which + 1) * 3 * TILE, :] = jnp.concatenate(
                [near, far_side, ratio], axis=0
            )
        for step in (2, 3, 1):
            slot_copy(phase, spot ^ step).start()
        plane_inbox[phase, spot] = outboxes[phase][parcel(spot), :]

    index_copy.wait()

    def done(step):
        return jnp.maximum(0, jnp.minimum(2 * (step - START), step - LAG))

    def ready(phase):
        return max((phase + 1) * steps + LAG - 1, -(-(phase + 1) * steps // 2) + START - 1)

    @pl.loop(0, chunks + LAG)
    def _(step):
        @pl.when(step < chunks)
        def _():
            forward(step)

        @pl.when(step == START)
        def _():
            @pl.loop(0, planes)
            def _(source):
                height_arrival(source).wait_recv()

        @pl.loop(done(step), done(step + 1))
        def _(chunk):
            compute(chunk)

        for phase in range(early):
            @pl.when(step == ready(phase))
            def _():
                unit_start(phase)

    size = len(places) * CAP
    for at, piece in enumerate(split(sums[early] * scale, PIECES)):
        stack[at * LINES:(at + 1) * LINES, :] = piece
    chosen[...] = jnp.dot(picks[...], stack[...], preferred_element_type=jnp.float32)

    @pl.loop(0, devices // BAND)
    def _(some):
        for one in range(BAND):
            which = some * BAND + one
            near, far_side, first_power, second_power = (
                chosen[pl.ds(pl.multiple_of(which * size + at * TILE, TILE), TILE), :] for at in range(4)
            )
            for at, value in enumerate((near, far_side, ratio_of(near, far_side, first_power, second_power))):
                outbox[which, at] = value

    def peer(step):
        return lax.rem(me + step, devices)

    def out_copy(to):
        return pltpu.make_async_remote_copy(
            src_ref=outbox.at[to],
            dst_ref=inbox.at[me],
            send_sem=out_send.at[to],
            recv_sem=out_recv.at[me],
            device_id={"date": to},
        )

    def out_arrival(source):
        return pltpu.make_async_remote_copy(
            src_ref=outbox.at[source],
            dst_ref=inbox.at[source],
            send_sem=out_send.at[source],
            recv_sem=out_recv.at[source],
            device_id={"date": source},
        )

    @pl.loop(1, devices)
    def _(step):
        out_copy(peer(step)).start()

    inbox[me] = outbox[me]

    for phase in range(early):
        @pl.loop(1, planes)
        def _(turn):
            unit_arrival(phase, other_plane(turn)).wait_recv()

        choose(phase)

    @pl.loop(0, planes)
    def _(to_plane):
        @pl.when(to_plane * BAND + reader != me)
        def _():
            height_copy(to_plane).wait_send()

    @pl.loop(0, chunks)
    def _(chunk):
        for upper in range(2):
            plane_all(upper, chunk).wait_send()

            @pl.when(relays[upper])
            def _():
                relay_all(upper, chunk).wait_send()

    for phase in range(early):
        for step in range(1, BAND):
            slot_arrival(phase, spot ^ step).wait_recv()

    @pl.loop(1, devices)
    def _(step):
        out_arrival(peer(step)).wait_recv()

    looks = coherence_out.shape[0] // CAP
    left = lax.broadcasted_iota(jnp.int32, (TILE, LANES), 1) < part_lanes
    for quarter in range(BAND):
        for tile in range(tiles):
            for part in range(3):
                sides = []
                for half in range(HALVES):
                    phase = tile * HALVES + half
                    if phase < early:
                        sides.append(plane_inbox[phase, quarter, part * TILE:(part + 1) * TILE, :])
                    else:
                        value = inbox[quarter, part]
                        for other in range(1, planes):
                            value = value + inbox[other * BAND + quarter, part]
                        sides.append(value)
                here, there = sides
                values = (
                    jnp.where(left, here, pltpu.roll(there, part_lanes, 1)),
                    jnp.where(left, pltpu.roll(here, part_lanes, 1), there),
                )
                for look_row, value in enumerate(values):
                    for c in range(2):
                        upper = 1 - part if part < 2 else 1 - c
                        at = ((quarter * 2 + upper) * tiles + tile) * look_rows + look_row
                        piece = value[c * CAP:(c + 1) * CAP]
                        if part < 2:
                            looks_out[pl.ds(c * looks + at, CAP, stride=2 * looks), :] = piece
                        else:
                            coherence_out[pl.ds(at, CAP, stride=looks), :] = piece

    for phase in range(early):
        @pl.loop(1, planes)
        def _(turn):
            unit_copy(phase, other_plane(turn)).wait_send()

        for step in range(1, BAND):
            slot_copy(phase, spot ^ step).wait_send()

    @pl.loop(1, devices)
    def _(step):
        out_copy(peer(step)).wait_send()


def body(images, height_phase, baseline, pair_list, pair_owner):
    devices = lax.axis_size("date")
    rows, columns = images.shape[2:]
    lanes = columns // LOOK_COLS
    looks = rows // LOOK_ROWS
    planes = devices // BAND
    tiles = rows // (2 * BAND * TILE)
    phases = tiles * HALVES
    early = phases - 1
    chunks = phases * (columns // (HALVES * LANES * WIDE))
    dates = 2 * BAND
    pairs = pair_list.shape[0]
    assert lanes == LANES and rows == LOOK_ROWS * devices and TILE == 2 * LOOK_ROWS and HALVES == 2
    assert rows % (2 * BAND * TILE) == 0 and columns % (HALVES * LANES * WIDE) == 0
    assert PIECES * LINES <= DEPTH
    vmem = pl.BlockSpec(memory_space=pltpu.VMEM)
    hbm = pl.BlockSpec(memory_space=pltpu.HBM)
    dma = pltpu.SemaphoreType.DMA
    tiled = images[0].reshape(2, rows // TILE, TILE, columns // LANES, LANES).transpose(0, 1, 3, 2, 4)
    inputs = [
        pltpu.with_memory_space_constraint(v, pltpu.HBM)
        for v in (tiled, height_phase, baseline[None], pair_list.T, pair_owner.T)
    ]
    scratch = [
        pltpu.VMEM((2, chunks, 2, WIDE, dates * TILE, LANES), jnp.float32),
        pltpu.VMEM((planes, LOOK_ROWS, columns), jnp.float32),
        pltpu.VMEM((2 * columns // HALVES, lanes), jnp.bfloat16),
        pltpu.VMEM((phases, LINES, lanes), jnp.float32),
        pltpu.VMEM((devices * TILE * CAP, DEPTH), jnp.bfloat16),
        pltpu.VMEM((DEPTH, lanes), jnp.bfloat16),
        pltpu.VMEM((devices * TILE * CAP, lanes), jnp.float32),
        pltpu.VMEM((devices, 3, TILE, lanes), jnp.float32),
        pltpu.VMEM((devices, 3, TILE, lanes), jnp.float32),
        pltpu.VMEM((1, devices), jnp.float32),
        pltpu.VMEM((2, pairs), jnp.int32),
        pltpu.VMEM((1, pairs), jnp.int32),
        pltpu.VMEM((BAND * CAP, LANES), jnp.int32),
        pltpu.SMEM((BAND * CAP, LANES), jnp.int32),
        pltpu.VMEM((early, BAND * 4 * TILE, lanes), jnp.float32),
        pltpu.VMEM((early, BAND, 3 * TILE, lanes), jnp.float32),
    ]
    scratch += [pltpu.VMEM((planes * UNIT + TILE, lanes), jnp.float32)] * early
    scratch += [pltpu.VMEM((BAND * 3 * TILE, lanes), jnp.float32)] * early
    size = sum(math.prod(s.shape) * jnp.dtype(s.dtype).itemsize for s in scratch)
    scratch += [
        pltpu.SemaphoreType.REGULAR((planes - 1,)),
        dma((4,)),
        dma((2, chunks)),
        dma((2, chunks)),
        dma((2, chunks, BAND)),
        dma((2, chunks)),
        dma((planes,)),
        dma((planes,)),
        dma((early, planes)),
        dma((early, planes)),
        dma((early, BAND)),
        dma((early, BAND)),
        dma((devices,)),
        dma((devices,)),
    ]
    look, coherence = pl.pallas_call(
        functools.partial(kernel, devices, phases),
        out_shape=(
            jax.ShapeDtypeStruct((CAP * 2 * looks, lanes), jnp.float32),
            jax.ShapeDtypeStruct((CAP * looks, lanes), jnp.float32),
        ),
        in_specs=[hbm] * 5,
        out_specs=(vmem, vmem),
        scratch_shapes=scratch,
        compiler_params=pltpu.CompilerParams(
            collective_id=0, has_side_effects=True, vmem_limit_bytes=size + (6 << 20)
        ),
    )(*inputs)
    return look.reshape(CAP, 2, looks, lanes), coherence.reshape(CAP, looks, lanes)


def solution(mesh):
    in_specs = (
        P(("groups", "date"), None, None, None),
        P(("groups", "date"), None),
        P("groups"),
        P(),
        P(),
    )
    out_specs = (P(("groups", "date"), None, None, None), P(("groups", "date"), None, None))
    return jax.shard_map(body, mesh=mesh, in_specs=in_specs, out_specs=out_specs, check_vma=False)
```

```python
import functools
import math

import jax
import jax.numpy as jnp
from jax import lax
from jax.experimental import pallas as pl
from jax.experimental.pallas import tpu as pltpu
from jax.sharding import PartitionSpec as P

LOOK_ROWS = 4
LOOK_COLS = 20
CAP = 4
BAND = 4
EPSILON = 1e-06
LANES = 128
TILE = 8
HALVES = 2
QUANTITIES = 2 + 2 * BAND
LINES = QUANTITIES * TILE
UNIT = LINES - TILE
PARTS = 8
PIECES = 3
DEPTH = 256
FIRST = 1
LAG = 3


def split(values, parts):
    pieces = []
    for _ in range(parts):
        piece = values.astype(jnp.bfloat16)
        pieces.append(piece)
        values = values - piece.astype(jnp.float32)
    return pieces


def cos_sin(angle):
    square = angle * angle
    sine = jnp.full_like(angle, -1.0 / math.factorial(15))
    for term in range(6, -1, -1):
        sine = sine * square + (-1.0) ** term / math.factorial(2 * term + 1)
    cosine = jnp.full_like(angle, 1.0 / math.factorial(16))
    for term in range(7, -1, -1):
        cosine = cosine * square + (-1.0) ** term / math.factorial(2 * term)
    return cosine, sine * angle


def chunk_list(phases, blocks):
    chunks = []
    for phase in range(phases):
        widths = [blocks - blocks // 2, blocks // 2] if phase < phases - 1 else [blocks - 5, 3, 2]
        start = phase * blocks
        for width in widths:
            chunks.append((start, width))
            start += width
    return chunks


def kernel(
    devices, phases, images, height, baseline_in, pair_list_in, pair_owner_in, looks_out, coherence_out,
    window, heights, box, sums, picks, stack, chosen, outbox, inbox, baseline, pair_list, pair_owner,
    table, index, staged, plane_inbox, *rest,
):
    early = phases - 1
    units, outboxes = rest[:early], rest[early:2 * early]
    (
        far, small_sem, plane_send, relay_send, plane_recv, relay_recv, height_send, height_recv, height_relay_send,
        unit_send, unit_recv, slot_send, slot_recv, out_send, out_recv,
    ) = rest[2 * early:]
    me = lax.axis_index("date")
    planes = devices // BAND
    plane = lax.div(me, BAND)
    spot = lax.rem(me, BAND)
    tiles = phases // HALVES
    column_tiles = images.shape[2]
    columns = column_tiles * LANES
    part_columns = columns // HALVES
    steps = part_columns // LANES
    chunks = chunk_list(phases, steps)
    side = BAND * TILE
    dates = 2 * BAND
    part_lanes = LANES // HALVES
    look_rows = TILE // LOOK_ROWS
    below, above = plane > 0, plane < planes - 1

    barrier = pltpu.get_barrier_semaphore()

    def hello(to):
        pl.semaphore_signal(barrier, inc=1, device_id={"date": to})

    for step in range(1, BAND):
        hello(plane * BAND + (spot ^ step))

    @pl.when(below)
    def _():
        hello(me - BAND)

    @pl.when(above)
    def _():
        hello(me + BAND)

    reader = spot - lax.rem(spot, look_rows) + lax.rem(plane, 2)
    own_height = lax.div(plane, 2) * look_rows + lax.rem(spot, look_rows)

    def small_copies():
        return [
            pltpu.make_async_copy(source, to, small_sem.at[at])
            for at, (source, to) in enumerate(
                ((baseline_in, baseline), (pair_list_in, pair_list), (pair_owner_in, pair_owner))
            )
        ]

    def height_copy(to_plane):
        return pltpu.make_async_remote_copy(
            src_ref=height,
            dst_ref=heights.at[own_height],
            send_sem=height_send.at[to_plane],
            recv_sem=height_recv.at[own_height],
            device_id={"date": to_plane * BAND + reader},
        )

    def height_own():
        return pltpu.make_async_copy(height, heights.at[own_height], height_recv.at[own_height])

    def height_arrival(source):
        return pltpu.make_async_remote_copy(
            src_ref=height,
            dst_ref=heights.at[source],
            send_sem=height_send.at[0],
            recv_sem=height_recv.at[source],
            device_id={"date": me},
        )

    def tile_of(quarter, upper, tile):
        return (quarter >> 1) + 2 * ((quarter & 1) + 2 * (upper * tiles + tile))

    def lines(quarter, upper, chunk):
        start, width = chunks[chunk]
        tile = tile_of(quarter, upper, start // (steps * HALVES))
        return images.at[:, tile, start % (steps * HALVES):start % (steps * HALVES) + width]

    def place(upper, chunk, slot, size=TILE):
        start, width = chunks[chunk]
        return window.at[upper, :, start:start + width, pl.ds(pl.multiple_of(slot * TILE, TILE), size), :]

    def own_slot(upper, which):
        return (1 - upper) * BAND + which

    def plane_copy(step, upper, chunk):
        to = spot ^ step
        return pltpu.make_async_remote_copy(
            src_ref=lines(to, upper, chunk),
            dst_ref=place(upper, chunk, own_slot(upper, spot)),
            send_sem=plane_send.at[upper, chunk],
            recv_sem=plane_recv.at[upper, chunk, spot],
            device_id={"date": plane * BAND + to},
        )

    def plane_arrival(step, upper, chunk):
        source = spot ^ step
        return pltpu.make_async_remote_copy(
            src_ref=lines(source, upper, chunk),
            dst_ref=place(upper, chunk, own_slot(upper, source)),
            send_sem=plane_send.at[upper, chunk],
            recv_sem=plane_recv.at[upper, chunk, source],
            device_id={"date": plane * BAND + source},
        )

    def own_copy(upper, chunk):
        return pltpu.make_async_copy(
            lines(spot, upper, chunk),
            place(upper, chunk, own_slot(upper, spot)),
            plane_recv.at[upper, chunk, spot],
        )

    relays = (above, below)
    gets_relays = (below, above)

    def relay_copy(upper, chunk, which, source):
        return pltpu.make_async_remote_copy(
            src_ref=source,
            dst_ref=place(upper, chunk, upper * BAND + which),
            send_sem=relay_send.at[upper, chunk],
            recv_sem=relay_recv.at[upper, chunk],
            device_id={"date": me + BAND * (1 - 2 * upper)},
        )

    def relay_all(upper, chunk):
        return pltpu.make_async_remote_copy(
            src_ref=place(upper, chunk, (1 - upper) * BAND, side),
            dst_ref=place(upper, chunk, upper * BAND, side),
            send_sem=relay_send.at[upper, chunk],
            recv_sem=relay_recv.at[upper, chunk],
            device_id={"date": me},
        )

    def plane_all(upper, chunk):
        return pltpu.make_async_remote_copy(
            src_ref=place(upper, chunk, 0, side - TILE),
            dst_ref=place(upper, chunk, 0, side - TILE),
            send_sem=plane_send.at[upper, chunk],
            recv_sem=relay_recv.at[upper, chunk],
            device_id={"date": me},
        )

    def own_relays(chunk):
        for upper in range(2):
            @pl.when(relays[upper])
            def _():
                relay_copy(upper, chunk, spot, lines(spot, upper, chunk)).start()

    for copy in small_copies():
        copy.start()
    pl.semaphore_wait(barrier, BAND - 1 + jnp.where(below, 1, 0) + jnp.where(above, 1, 0))

    def rows_out(chunk):
        for step in (2, 3, 1):
            for upper in range(2):
                plane_copy(step, upper, chunk).start()
        for upper in range(2):
            own_copy(upper, chunk).start()

    for chunk in range(FIRST):
        rows_out(chunk)

    def height_direct(to_plane):
        return (to_plane * BAND + reader != me) & (
            height_near(to_plane) | ((to_plane > 0) & (to_plane < planes - 1))
        )

    def height_near(to_plane):
        return (to_plane - plane < 2) & (plane - to_plane < 2)

    def meet(turn):
        @pl.when(below)
        def _():
            pl.semaphore_signal(far.at[turn], inc=1, device_id={"date": me - BAND})

        @pl.when(above)
        def _():
            pl.semaphore_signal(far.at[turn], inc=1, device_id={"date": me + BAND})

        pl.semaphore_wait(far.at[turn], jnp.where(below, 1, 0) + jnp.where(above, 1, 0))

    @pl.when(reader == spot)
    def _():
        height_own().start()

    meet(0)

    @pl.loop(0, planes)
    def _(to_plane):
        @pl.when(height_direct(to_plane) & height_near(to_plane))
        def _():
            height_copy(to_plane).start()

    for chunk in range(len(chunks)):
        own_relays(chunk)

    for turn in range(1, planes - 1):
        meet(turn)

    @pl.loop(0, planes)
    def _(to_plane):
        @pl.when(height_direct(to_plane) & jnp.logical_not(height_near(to_plane)))
        def _():
            height_copy(to_plane).start()

    for chunk in range(FIRST, len(chunks)):
        rows_out(chunk)

    for upper in range(2):
        @pl.when(jnp.logical_not(gets_relays[upper]))
        def _():
            @pl.loop(0, phases * steps)
            def _(block):
                window[upper, :, block, upper * side:(upper + 1) * side, :] = jnp.zeros(
                    (2, side, LANES), jnp.float32
                )

    @pl.loop(0, steps)
    def _(block):
        shape = (look_rows * LANES, LANES)
        line = lax.broadcasted_iota(jnp.int32, shape, 0)
        position = block * LANES + (line & (LANES - 1))
        target = lax.broadcasted_iota(jnp.int32, shape, 1) - jnp.where(line >= LANES, part_lanes, 0)
        target = target * LOOK_COLS
        box[pl.ds(pl.multiple_of(block * look_rows * LANES, look_rows * LANES), look_rows * LANES), :] = jnp.where(
            (position >= target) & (position < target + LOOK_COLS), 1.0, 0.0
        ).astype(jnp.bfloat16)

    sums[...] = jnp.zeros_like(sums)
    stack[...] = jnp.zeros_like(stack)

    for copy in small_copies():
        copy.wait()

    lane = lax.broadcasted_iota(jnp.int32, (dates, devices), 1)
    date = lax.broadcasted_iota(jnp.int32, (dates, devices), 0)
    scales = []
    for upper in range(2):
        chosen_date = lane == date + (plane - 1 + upper) * BAND
        scales.append(
            jnp.sum(jnp.where(chosen_date, baseline[...], 0.0), axis=1, keepdims=True)
        )

    owner = pair_owner[...]
    pairs = owner.shape[1]
    down = lax.broadcasted_iota(jnp.int32, (pairs, pairs), 0)
    across = lax.broadcasted_iota(jnp.int32, (pairs, pairs), 1)
    owner_column = jnp.sum(jnp.where(down == across, owner, 0), axis=1, keepdims=True)
    earlier = (owner_column == owner) & (down < across)
    slot_of = owner * CAP + jnp.sum(jnp.where(earlier, 1, 0), axis=0, keepdims=True)
    first, second = pair_list[0:1, :], pair_list[1:2, :]
    distance = second - first
    first_here = lax.div(first, BAND) == plane
    second_here = lax.div(second, BAND) == plane
    first_at = lax.rem(first, BAND)
    second_at = lax.rem(second, BAND)
    others = (QUANTITIES - 1) * TILE
    places = (
        (first_here, first_at + distance * TILE),
        (first_here, first_at + (BAND + distance) * TILE),
        (second_here, second_at + distance * TILE + BAND),
        (second_here, second_at + (BAND + distance) * TILE + BAND),
        (first_here, first_at),
        (second_here, jnp.where(first_here, first_at + BAND, others + first_at)),
        (first_here, jnp.where(second_here, second_at, others + second_at + BAND)),
        (second_here, second_at + BAND),
    )
    total = devices * len(places) * CAP
    line = lax.broadcasted_iota(jnp.int32, (total, pairs), 0)
    part = (line & (len(places) * CAP - 1)) - (line & (CAP - 1))
    taken = lax.div(line, len(places)) - lax.div(line & (len(places) * CAP - 1), len(places)) + (line & (CAP - 1)) == slot_of
    listed = jnp.full((total, pairs), -1, jnp.int32)
    for at, (valid, value) in enumerate(places):
        listed = jnp.where(taken & valid & (part == at * CAP), value, listed)
    listed = jnp.max(listed.astype(jnp.float32), axis=1, keepdims=True)
    depth = lax.broadcasted_iota(jnp.int32, (total, DEPTH), 1).astype(jnp.float32)
    hit = (depth == listed)
    for piece in range(1, PIECES):
        hit = hit | (depth == listed + piece * LINES)
    picks[...] = jnp.where(hit & (listed >= 0.0), 1.0, 0.0).astype(jnp.bfloat16)

    first_line = lax.div(first, BAND) * UNIT + first_at
    second_line = lax.div(second, BAND) * UNIT + second_at
    lines_of = (
        first_line + distance * TILE,
        first_line + (BAND + distance) * TILE,
        second_line + distance * TILE + BAND,
        second_line + (BAND + distance) * TILE + BAND,
        first_line,
        first_line + BAND,
        second_line,
        second_line + BAND,
    )
    slots = BAND * CAP
    empty = planes * UNIT
    slot = lax.broadcasted_iota(jnp.int32, (slots, pairs), 0) + plane * slots
    taken = slot == slot_of
    table_lane = lax.broadcasted_iota(jnp.int32, (slots, LANES), 1)
    entries = jnp.zeros((slots, LANES), jnp.int32)
    for at, value in enumerate(lines_of):
        listed = empty + jnp.sum(jnp.where(taken, value - empty, 0), axis=1, keepdims=True)
        entries = jnp.where(table_lane == at, listed, entries)
    table[...] = jnp.clip(entries, 0, empty)
    index_copy = pltpu.make_async_copy(table, index, small_sem.at[3])
    index_copy.start()
    for unit in units:
        unit[empty:, :] = jnp.zeros((TILE, LANES), jnp.float32)

    def forward(chunk):
        for step in (1, 2, 3):
            for upper in range(2):
                plane_arrival(step, upper, chunk).wait_recv()

                @pl.when(relays[upper])
                def _():
                    which = spot ^ step
                    relay_copy(
                        upper, chunk, which, place(upper, chunk, own_slot(upper, which))
                    ).start()

    def height_onward(source, up):
        origin = lax.div(source, look_rows) * 2 + lax.rem(spot, 2)
        if up:
            return (plane == planes - 2) & (origin < planes - 2)
        return (plane == 1) & (origin > 1)

    def height_relay(source, up):
        return pltpu.make_async_remote_copy(
            src_ref=heights.at[source],
            dst_ref=heights.at[source],
            send_sem=height_relay_send.at[up, source],
            recv_sem=height_recv.at[source],
            device_id={"date": me + BAND * (2 * up - 1)},
        )

    def height_pass():
        @pl.loop(0, planes)
        def _(source):
            for up in range(2):
                @pl.when(height_onward(source, up))
                def _():
                    height_arrival(source).wait_recv()
                    height_relay(source, up).start()

    own_rows = lax.broadcasted_iota(jnp.int32, (dates, LANES), 0) < BAND

    def compute(chunk):
        for upper in range(2):
            own_copy(upper, chunk).wait()

            @pl.when(gets_relays[upper])
            def _():
                relay_all(upper, chunk).wait_recv()

        start, width = chunks[chunk]

        @pl.loop(start, start + width)
        def _(block):
            phase = lax.div(block, steps)
            tile = lax.div(phase, HALVES)
            column = pl.multiple_of(lax.rem(block, steps * HALVES) * LANES, LANES)
            totals = []
            for look_row in range(look_rows):
                found = [None] * QUANTITIES

                def add(at, value):
                    found[at] = value if found[at] is None else found[at] + value

                for row in range(LOOK_ROWS):
                    flat = []
                    for upper in range(2):
                        source = (upper * tiles + tile) * look_rows + look_row
                        level = heights[source, row:row + 1, pl.ds(column, LANES)]
                        cosine, sine = cos_sin(scales[upper] * level)
                        at = pl.ds(look_row * LOOK_ROWS + row, dates, stride=TILE)
                        real = window[upper, 0, block, at, :]
                        imag = window[upper, 1, block, at, :]
                        flat.append((real * cosine - imag * sine, real * sine + imag * cosine))
                    own_real, own_imag = (jnp.where(own_rows, u, l) for l, u in zip(*flat))
                    add(0, own_real * own_real + own_imag * own_imag)
                    rest_real, rest_imag = (jnp.where(own_rows, l, u) for l, u in zip(*flat))
                    add(QUANTITIES - 1, rest_real * rest_real + rest_imag * rest_imag)
                    for distance in range(1, BAND + 1):
                        other_real, other_imag = (
                            jnp.where(
                                own_rows, pltpu.roll(u, dates - distance, 0), pltpu.roll(l, distance, 0)
                            )
                            for l, u in zip(*flat)
                        )
                        add(distance, own_real * other_real + own_imag * other_imag)
                        add(BAND + distance, own_imag * other_real - own_real * other_imag)
                totals.append(jnp.concatenate(found, axis=0))
            weights = box[
                pl.ds(pl.multiple_of(lax.rem(block, steps) * look_rows * LANES, LANES), look_rows * LANES), :
            ]
            summed = sums[phase]
            for piece in split(jnp.concatenate(totals, axis=1), 2):
                summed = summed + jnp.dot(piece, weights, preferred_element_type=jnp.float32)
            sums[phase] = summed

    line = lax.broadcasted_iota(jnp.int32, (LINES, LANES), 0)
    turned = (line >= (1 + BAND) * TILE) & (line < (1 + 2 * BAND) * TILE) & ((line & BAND) == BAND)
    scale = jnp.where(turned, -1.0, 1.0) * (1.0 / (LOOK_ROWS * LOOK_COLS))

    def unit_lines(phase, which):
        return units[phase].at[pl.ds(pl.multiple_of(which * UNIT, TILE), UNIT), :]

    def unit_copy(phase, to_plane):
        return pltpu.make_async_remote_copy(
            src_ref=unit_lines(phase, plane),
            dst_ref=unit_lines(phase, plane),
            send_sem=unit_send.at[phase, to_plane],
            recv_sem=unit_recv.at[phase, plane],
            device_id={"date": to_plane * BAND + spot},
        )

    def unit_arrival(phase, source):
        return pltpu.make_async_remote_copy(
            src_ref=unit_lines(phase, source),
            dst_ref=unit_lines(phase, source),
            send_sem=unit_send.at[phase, source],
            recv_sem=unit_recv.at[phase, source],
            device_id={"date": source * BAND + spot},
        )

    def other_plane(turn):
        return lax.rem(plane + turn, planes)

    def unit_start(phase):
        units[phase][pl.ds(pl.multiple_of(plane * UNIT, TILE), UNIT), :] = sums[phase, :UNIT] * scale[:UNIT]

        @pl.loop(1, planes)
        def _(turn):
            unit_copy(phase, other_plane(turn)).start()

    def ratio_of(near, far_side, first_power, second_power):
        squares = [v * v for v in (near, far_side)]
        squares = [v + pltpu.roll(v, CAP, 0) for v in squares]
        level = jnp.sqrt(jnp.where(own_rows, squares[0], squares[1]))
        return level / jnp.sqrt((first_power + EPSILON) * (second_power + EPSILON))

    def parcel(to):
        return pl.ds(pl.multiple_of(to * 3 * TILE, TILE), 3 * TILE)

    def slot_copy(phase, to):
        return pltpu.make_async_remote_copy(
            src_ref=outboxes[phase].at[parcel(to), :],
            dst_ref=plane_inbox.at[phase, spot],
            send_sem=slot_send.at[phase, to],
            recv_sem=slot_recv.at[phase, spot],
            device_id={"date": plane * BAND + to},
        )

    def slot_arrival(phase, source):
        return pltpu.make_async_remote_copy(
            src_ref=outboxes[phase].at[parcel(source), :],
            dst_ref=plane_inbox.at[phase, source],
            send_sem=slot_send.at[phase, source],
            recv_sem=slot_recv.at[phase, source],
            device_id={"date": plane * BAND + source},
        )

    def choose(phase):
        unit = units[phase]
        for which in range(BAND):
            for at in range(CAP):
                for part in range(PARTS):
                    line = jnp.clip(index[which * CAP + at, part], 0, planes * UNIT)
                    row = (which * 4 + part // 2) * TILE + part % 2 * CAP + at
                    staged[phase, row:row + 1, :] = unit[pl.ds(line, 1), :]
        for which in range(BAND):
            near, far_side, first_power, second_power = (
                staged[phase, (which * 4 + at) * TILE:(which * 4 + at + 1) * TILE, :] for at in range(4)
            )
            ratio = ratio_of(near, far_side, first_power, second_power)
            outboxes[phase][which * 3 * TILE:(which + 1) * 3 * TILE, :] = jnp.concatenate(
                [near, far_side, ratio], axis=0
            )
        for step in (2, 3, 1):
            slot_copy(phase, spot ^ step).start()
        plane_inbox[phase, spot] = outboxes[phase][parcel(spot), :]

    index_copy.wait()

    last = len(chunks) - 1
    computed = 0
    for chunk in range(len(chunks) + LAG):
        if chunk <= last:
            forward(chunk)
        if chunk == 0:
            height_pass()
        while computed <= min(chunk - LAG, last):
            if computed == 0:
                @pl.loop(0, planes)
                def _(source):
                    @pl.when(jnp.logical_not(height_onward(source, 0) | height_onward(source, 1)))
                    def _():
                        height_arrival(source).wait_recv()

            compute(computed)
            start, width = chunks[computed]
            if (start + width) % steps == 0 and computed < last:
                unit_start(start // steps)
            computed += 1

    size = len(places) * CAP
    for at, piece in enumerate(split(sums[early] * scale, PIECES)):
        stack[at * LINES:(at + 1) * LINES, :] = piece
    chosen[...] = jnp.dot(picks[...], stack[...], preferred_element_type=jnp.float32)

    @pl.loop(0, devices // BAND)
    def _(some):
        for one in range(BAND):
            which = some * BAND + one
            near, far_side, first_power, second_power = (
                chosen[pl.ds(pl.multiple_of(which * size + at * TILE, TILE), TILE), :] for at in range(4)
            )
            for at, value in enumerate((near, far_side, ratio_of(near, far_side, first_power, second_power))):
                outbox[which, at] = value

    def peer(step):
        return lax.rem(me + step, devices)

    def out_copy(to):
        return pltpu.make_async_remote_copy(
            src_ref=outbox.at[to],
            dst_ref=inbox.at[me],
            send_sem=out_send.at[to],
            recv_sem=out_recv.at[me],
            device_id={"date": to},
        )

    def out_arrival(source):
        return pltpu.make_async_remote_copy(
            src_ref=outbox.at[source],
            dst_ref=inbox.at[source],
            send_sem=out_send.at[source],
            recv_sem=out_recv.at[source],
            device_id={"date": source},
        )

    @pl.loop(1, devices)
    def _(step):
        out_copy(peer(step)).start()

    inbox[me] = outbox[me]

    for phase in range(early):
        @pl.loop(1, planes)
        def _(turn):
            unit_arrival(phase, other_plane(turn)).wait_recv()

        choose(phase)

    @pl.loop(0, planes)
    def _(to_plane):
        @pl.when(height_direct(to_plane))
        def _():
            height_copy(to_plane).wait_send()

    @pl.loop(0, planes)
    def _(source):
        for up in range(2):
            @pl.when(height_onward(source, up))
            def _():
                height_relay(source, up).wait_send()

    for chunk in range(len(chunks)):
        for upper in range(2):
            plane_all(upper, chunk).wait_send()

            @pl.when(relays[upper])
            def _():
                relay_all(upper, chunk).wait_send()

    for phase in range(early):
        for step in range(1, BAND):
            slot_arrival(phase, spot ^ step).wait_recv()

    @pl.loop(1, devices)
    def _(step):
        out_arrival(peer(step)).wait_recv()

    looks = coherence_out.shape[0] // CAP
    left = lax.broadcasted_iota(jnp.int32, (TILE, LANES), 1) < part_lanes
    for quarter in range(BAND):
        for tile in range(tiles):
            for part in range(3):
                sides = []
                for half in range(HALVES):
                    phase = tile * HALVES + half
                    if phase < early:
                        sides.append(plane_inbox[phase, quarter, part * TILE:(part + 1) * TILE, :])
                    else:
                        value = inbox[quarter, part]
                        for other in range(1, planes):
                            value = value + inbox[other * BAND + quarter, part]
                        sides.append(value)
                here, there = sides
                values = (
                    jnp.where(left, here, pltpu.roll(there, part_lanes, 1)),
                    jnp.where(left, pltpu.roll(here, part_lanes, 1), there),
                )
                for look_row, value in enumerate(values):
                    for c in range(2):
                        upper = 1 - part if part < 2 else 1 - c
                        at = tile_of(quarter, upper, tile) * look_rows + look_row
                        piece = value[c * CAP:(c + 1) * CAP]
                        if part < 2:
                            looks_out[pl.ds(c * looks + at, CAP, stride=2 * looks), :] = piece
                        else:
                            coherence_out[pl.ds(at, CAP, stride=looks), :] = piece

    for phase in range(early):
        @pl.loop(1, planes)
        def _(turn):
            unit_copy(phase, other_plane(turn)).wait_send()

        for step in range(1, BAND):
            slot_copy(phase, spot ^ step).wait_send()

    @pl.loop(1, devices)
    def _(step):
        out_copy(peer(step)).wait_send()


def body(images, height_phase, baseline, pair_list, pair_owner):
    devices = lax.axis_size("date")
    rows, columns = images.shape[2:]
    lanes = columns // LOOK_COLS
    looks = rows // LOOK_ROWS
    planes = devices // BAND
    tiles = rows // (2 * BAND * TILE)
    phases = tiles * HALVES
    early = phases - 1
    blocks = columns // (HALVES * LANES)
    chunks = len(chunk_list(phases, blocks))
    dates = 2 * BAND
    pairs = pair_list.shape[0]
    assert lanes == LANES and rows == LOOK_ROWS * devices and TILE == 2 * LOOK_ROWS and HALVES == 2
    assert rows % (2 * BAND * TILE) == 0 and columns % (HALVES * LANES) == 0 and blocks > 5
    assert PIECES * LINES <= DEPTH
    vmem = pl.BlockSpec(memory_space=pltpu.VMEM)
    hbm = pl.BlockSpec(memory_space=pltpu.HBM)
    dma = pltpu.SemaphoreType.DMA
    tiled = images[0].reshape(2, rows // TILE, TILE, columns // LANES, LANES).transpose(0, 1, 3, 2, 4)
    inputs = [
        pltpu.with_memory_space_constraint(v, pltpu.HBM)
        for v in (tiled, height_phase, baseline[None], pair_list.T, pair_owner.T)
    ]
    scratch = [
        pltpu.VMEM((2, 2, phases * blocks, dates * TILE, LANES), jnp.float32),
        pltpu.VMEM((planes, LOOK_ROWS, columns), jnp.float32),
        pltpu.VMEM((2 * columns // HALVES, lanes), jnp.bfloat16),
        pltpu.VMEM((phases, LINES, lanes), jnp.float32),
        pltpu.VMEM((devices * TILE * CAP, DEPTH), jnp.bfloat16),
        pltpu.VMEM((DEPTH, lanes), jnp.bfloat16),
        pltpu.VMEM((devices * TILE * CAP, lanes), jnp.float32),
        pltpu.VMEM((devices, 3, TILE, lanes), jnp.float32),
        pltpu.VMEM((devices, 3, TILE, lanes), jnp.float32),
        pltpu.VMEM((1, devices), jnp.float32),
        pltpu.VMEM((2, pairs), jnp.int32),
        pltpu.VMEM((1, pairs), jnp.int32),
        pltpu.VMEM((BAND * CAP, LANES), jnp.int32),
        pltpu.SMEM((BAND * CAP, LANES), jnp.int32),
        pltpu.VMEM((early, BAND * 4 * TILE, lanes), jnp.float32),
        pltpu.VMEM((early, BAND, 3 * TILE, lanes), jnp.float32),
    ]
    scratch += [pltpu.VMEM((planes * UNIT + TILE, lanes), jnp.float32)] * early
    scratch += [pltpu.VMEM((BAND * 3 * TILE, lanes), jnp.float32)] * early
    size = sum(math.prod(s.shape) * jnp.dtype(s.dtype).itemsize for s in scratch)
    scratch += [
        pltpu.SemaphoreType.REGULAR((planes - 1,)),
        dma((4,)),
        dma((2, chunks)),
        dma((2, chunks)),
        dma((2, chunks, BAND)),
        dma((2, chunks)),
        dma((planes,)),
        dma((planes,)),
        dma((2, planes)),
        dma((early, planes)),
        dma((early, planes)),
        dma((early, BAND)),
        dma((early, BAND)),
        dma((devices,)),
        dma((devices,)),
    ]
    look, coherence = pl.pallas_call(
        functools.partial(kernel, devices, phases),
        out_shape=(
            jax.ShapeDtypeStruct((CAP * 2 * looks, lanes), jnp.float32),
            jax.ShapeDtypeStruct((CAP * looks, lanes), jnp.float32),
        ),
        in_specs=[hbm] * 5,
        out_specs=(vmem, vmem),
        scratch_shapes=scratch,
        compiler_params=pltpu.CompilerParams(
            collective_id=0, has_side_effects=True, vmem_limit_bytes=size + (6 << 20)
        ),
    )(*inputs)
    return look.reshape(CAP, 2, looks, lanes), coherence.reshape(CAP, looks, lanes)


def solution(mesh):
    in_specs = (
        P(("groups", "date"), None, None, None),
        P(("groups", "date"), None),
        P("groups"),
        P(),
        P(),
    )
    out_specs = (P(("groups", "date"), None, None, None), P(("groups", "date"), None, None))
    return jax.shard_map(body, mesh=mesh, in_specs=in_specs, out_specs=out_specs, check_vma=False)
```

```python
import functools
import math

import jax
import jax.numpy as jnp
from jax import lax
from jax.experimental import pallas as pl
from jax.experimental.pallas import tpu as pltpu
from jax.sharding import PartitionSpec as P

LOOK_ROWS = 4
LOOK_COLS = 20
CAP = 4
BAND = 4
EPSILON = 1e-06
LANES = 128
TILE = 8
HALVES = 2
QUANTITIES = 2 + 2 * BAND
LINES = QUANTITIES * TILE
UNIT = LINES - TILE
PARTS = 8
PIECES = 3
DEPTH = 256
FIRST = 1
LAG = 3


def split(values, parts):
    pieces = []
    for _ in range(parts):
        piece = values.astype(jnp.bfloat16)
        pieces.append(piece)
        values = values - piece.astype(jnp.float32)
    return pieces


def cos_sin(angle):
    square = angle * angle
    sine = jnp.full_like(angle, -1.0 / math.factorial(15))
    for term in range(6, -1, -1):
        sine = sine * square + (-1.0) ** term / math.factorial(2 * term + 1)
    cosine = jnp.full_like(angle, 1.0 / math.factorial(16))
    for term in range(7, -1, -1):
        cosine = cosine * square + (-1.0) ** term / math.factorial(2 * term)
    return cosine, sine * angle


def chunk_list(phases, blocks):
    chunks = []
    for phase in range(phases):
        widths = [blocks - blocks // 2, blocks // 2] if phase < phases - 1 else [blocks - 5, 3, 2]
        start = phase * blocks
        for width in widths:
            chunks.append((start, width))
            start += width
    return chunks


def tile_of(tiles, quarter, upper, tile):
    return (quarter >> 1) + 2 * ((quarter & 1) + 2 * (upper * tiles + tile))


def kernel(
    devices, phases, images, height, baseline_in, pair_list_in, pair_owner_in, inbox, plane_inbox,
    window, heights, box, sums, picks, stack, chosen, outbox, baseline, pair_list, pair_owner,
    table, index, staged, *rest,
):
    early = phases - 1
    units, outboxes = rest[:early], rest[early:2 * early]
    (
        far, small_sem, plane_send, relay_send, plane_recv, relay_recv, height_send, height_recv, height_relay_send,
        unit_send, unit_recv, slot_send, slot_recv, out_send, out_recv,
    ) = rest[2 * early:]
    me = lax.axis_index("date")
    planes = devices // BAND
    plane = lax.div(me, BAND)
    spot = lax.rem(me, BAND)
    tiles = phases // HALVES
    column_tiles = images.shape[2]
    columns = column_tiles * LANES
    part_columns = columns // HALVES
    steps = part_columns // LANES
    chunks = chunk_list(phases, steps)
    side = BAND * TILE
    dates = 2 * BAND
    part_lanes = LANES // HALVES
    look_rows = TILE // LOOK_ROWS
    below, above = plane > 0, plane < planes - 1

    barrier = pltpu.get_barrier_semaphore()

    def hello(to):
        pl.semaphore_signal(barrier, inc=1, device_id={"date": to})

    for step in range(1, BAND):
        hello(plane * BAND + (spot ^ step))

    @pl.when(below)
    def _():
        hello(me - BAND)

    @pl.when(above)
    def _():
        hello(me + BAND)

    reader = spot - lax.rem(spot, look_rows) + lax.rem(plane, 2)
    own_height = lax.div(plane, 2) * look_rows + lax.rem(spot, look_rows)

    def small_copies():
        return [
            pltpu.make_async_copy(source, to, small_sem.at[at])
            for at, (source, to) in enumerate(
                ((baseline_in, baseline), (pair_list_in, pair_list), (pair_owner_in, pair_owner))
            )
        ]

    def height_copy(to_plane):
        return pltpu.make_async_remote_copy(
            src_ref=height,
            dst_ref=heights.at[own_height],
            send_sem=height_send.at[to_plane],
            recv_sem=height_recv.at[own_height],
            device_id={"date": to_plane * BAND + reader},
        )

    def height_own():
        return pltpu.make_async_copy(height, heights.at[own_height], height_recv.at[own_height])

    def height_arrival(source):
        return pltpu.make_async_remote_copy(
            src_ref=height,
            dst_ref=heights.at[source],
            send_sem=height_send.at[0],
            recv_sem=height_recv.at[source],
            device_id={"date": me},
        )

    def lines(quarter, upper, chunk):
        start, width = chunks[chunk]
        tile = tile_of(tiles, quarter, upper, start // (steps * HALVES))
        return images.at[:, tile, start % (steps * HALVES):start % (steps * HALVES) + width]

    def place(upper, chunk, slot, size=TILE):
        start, width = chunks[chunk]
        return window.at[upper, :, start:start + width, pl.ds(pl.multiple_of(slot * TILE, TILE), size), :]

    def own_slot(upper, which):
        return (1 - upper) * BAND + which

    def plane_copy(step, upper, chunk):
        to = spot ^ step
        return pltpu.make_async_remote_copy(
            src_ref=lines(to, upper, chunk),
            dst_ref=place(upper, chunk, own_slot(upper, spot)),
            send_sem=plane_send.at[upper, chunk],
            recv_sem=plane_recv.at[upper, chunk, spot],
            device_id={"date": plane * BAND + to},
        )

    def plane_arrival(step, upper, chunk):
        source = spot ^ step
        return pltpu.make_async_remote_copy(
            src_ref=lines(source, upper, chunk),
            dst_ref=place(upper, chunk, own_slot(upper, source)),
            send_sem=plane_send.at[upper, chunk],
            recv_sem=plane_recv.at[upper, chunk, source],
            device_id={"date": plane * BAND + source},
        )

    def own_copy(upper, chunk):
        return pltpu.make_async_copy(
            lines(spot, upper, chunk),
            place(upper, chunk, own_slot(upper, spot)),
            plane_recv.at[upper, chunk, spot],
        )

    relays = (above, below)
    gets_relays = (below, above)

    def relay_copy(upper, chunk, which, source):
        return pltpu.make_async_remote_copy(
            src_ref=source,
            dst_ref=place(upper, chunk, upper * BAND + which),
            send_sem=relay_send.at[upper, chunk],
            recv_sem=relay_recv.at[upper, chunk],
            device_id={"date": me + BAND * (1 - 2 * upper)},
        )

    def relay_all(upper, chunk):
        return pltpu.make_async_remote_copy(
            src_ref=place(upper, chunk, (1 - upper) * BAND, side),
            dst_ref=place(upper, chunk, upper * BAND, side),
            send_sem=relay_send.at[upper, chunk],
            recv_sem=relay_recv.at[upper, chunk],
            device_id={"date": me},
        )

    def plane_all(upper, chunk):
        return pltpu.make_async_remote_copy(
            src_ref=place(upper, chunk, 0, side - TILE),
            dst_ref=place(upper, chunk, 0, side - TILE),
            send_sem=plane_send.at[upper, chunk],
            recv_sem=relay_recv.at[upper, chunk],
            device_id={"date": me},
        )

    def own_relays(chunk):
        for upper in range(2):
            @pl.when(relays[upper])
            def _():
                relay_copy(upper, chunk, spot, lines(spot, upper, chunk)).start()

    for copy in small_copies():
        copy.start()
    pl.semaphore_wait(barrier, BAND - 1 + jnp.where(below, 1, 0) + jnp.where(above, 1, 0))

    def rows_out(chunk):
        for step in (2, 3, 1):
            for upper in range(2):
                plane_copy(step, upper, chunk).start()
        for upper in range(2):
            own_copy(upper, chunk).start()

    for chunk in range(FIRST):
        rows_out(chunk)

    def height_direct(to_plane):
        return (to_plane * BAND + reader != me) & (
            height_near(to_plane) | ((to_plane > 0) & (to_plane < planes - 1))
        )

    def height_near(to_plane):
        return (to_plane - plane < 2) & (plane - to_plane < 2)

    def meet(turn):
        @pl.when(below)
        def _():
            pl.semaphore_signal(far.at[turn], inc=1, device_id={"date": me - BAND})

        @pl.when(above)
        def _():
            pl.semaphore_signal(far.at[turn], inc=1, device_id={"date": me + BAND})

        pl.semaphore_wait(far.at[turn], jnp.where(below, 1, 0) + jnp.where(above, 1, 0))

    @pl.when(reader == spot)
    def _():
        height_own().start()

    meet(0)

    @pl.loop(0, planes)
    def _(to_plane):
        @pl.when(height_direct(to_plane) & height_near(to_plane))
        def _():
            height_copy(to_plane).start()

    for chunk in range(len(chunks)):
        own_relays(chunk)

    for turn in range(1, planes - 1):
        meet(turn)

    @pl.loop(0, planes)
    def _(to_plane):
        @pl.when(height_direct(to_plane) & jnp.logical_not(height_near(to_plane)))
        def _():
            height_copy(to_plane).start()

    for chunk in range(FIRST, len(chunks)):
        rows_out(chunk)

    for upper in range(2):
        @pl.when(jnp.logical_not(gets_relays[upper]))
        def _():
            @pl.loop(0, phases * steps)
            def _(block):
                window[upper, :, block, upper * side:(upper + 1) * side, :] = jnp.zeros(
                    (2, side, LANES), jnp.float32
                )

    @pl.loop(0, steps)
    def _(block):
        shape = (look_rows * LANES, LANES)
        line = lax.broadcasted_iota(jnp.int32, shape, 0)
        position = block * LANES + (line & (LANES - 1))
        target = lax.broadcasted_iota(jnp.int32, shape, 1) - jnp.where(line >= LANES, part_lanes, 0)
        target = target * LOOK_COLS
        box[pl.ds(pl.multiple_of(block * look_rows * LANES, look_rows * LANES), look_rows * LANES), :] = jnp.where(
            (position >= target) & (position < target + LOOK_COLS), 1.0, 0.0
        ).astype(jnp.bfloat16)

    sums[...] = jnp.zeros_like(sums)
    stack[...] = jnp.zeros_like(stack)

    for copy in small_copies():
        copy.wait()

    lane = lax.broadcasted_iota(jnp.int32, (dates, devices), 1)
    date = lax.broadcasted_iota(jnp.int32, (dates, devices), 0)
    scales = []
    for upper in range(2):
        chosen_date = lane == date + (plane - 1 + upper) * BAND
        scales.append(
            jnp.sum(jnp.where(chosen_date, baseline[...], 0.0), axis=1, keepdims=True)
        )

    owner = pair_owner[...]
    pairs = owner.shape[1]
    down = lax.broadcasted_iota(jnp.int32, (pairs, pairs), 0)
    across = lax.broadcasted_iota(jnp.int32, (pairs, pairs), 1)
    owner_column = jnp.sum(jnp.where(down == across, owner, 0), axis=1, keepdims=True)
    earlier = (owner_column == owner) & (down < across)
    slot_of = owner * CAP + jnp.sum(jnp.where(earlier, 1, 0), axis=0, keepdims=True)
    first, second = pair_list[0:1, :], pair_list[1:2, :]
    distance = second - first
    first_here = lax.div(first, BAND) == plane
    second_here = lax.div(second, BAND) == plane
    first_at = lax.rem(first, BAND)
    second_at = lax.rem(second, BAND)
    others = (QUANTITIES - 1) * TILE
    places = (
        (first_here, first_at + distance * TILE),
        (first_here, first_at + (BAND + distance) * TILE),
        (second_here, second_at + distance * TILE + BAND),
        (second_here, second_at + (BAND + distance) * TILE + BAND),
        (first_here, first_at),
        (second_here, jnp.where(first_here, first_at + BAND, others + first_at)),
        (first_here, jnp.where(second_here, second_at, others + second_at + BAND)),
        (second_here, second_at + BAND),
    )
    total = devices * len(places) * CAP
    line = lax.broadcasted_iota(jnp.int32, (total, pairs), 0)
    part = (line & (len(places) * CAP - 1)) - (line & (CAP - 1))
    taken = lax.div(line, len(places)) - lax.div(line & (len(places) * CAP - 1), len(places)) + (line & (CAP - 1)) == slot_of
    listed = jnp.full((total, pairs), -1, jnp.int32)
    for at, (valid, value) in enumerate(places):
        listed = jnp.where(taken & valid & (part == at * CAP), value, listed)
    listed = jnp.max(listed.astype(jnp.float32), axis=1, keepdims=True)
    depth = lax.broadcasted_iota(jnp.int32, (total, DEPTH), 1).astype(jnp.float32)
    hit = (depth == listed)
    for piece in range(1, PIECES):
        hit = hit | (depth == listed + piece * LINES)
    picks[...] = jnp.where(hit & (listed >= 0.0), 1.0, 0.0).astype(jnp.bfloat16)

    first_line = lax.div(first, BAND) * UNIT + first_at
    second_line = lax.div(second, BAND) * UNIT + second_at
    lines_of = (
        first_line + distance * TILE,
        first_line + (BAND + distance) * TILE,
        second_line + distance * TILE + BAND,
        second_line + (BAND + distance) * TILE + BAND,
        first_line,
        first_line + BAND,
        second_line,
        second_line + BAND,
    )
    slots = BAND * CAP
    empty = planes * UNIT
    slot = lax.broadcasted_iota(jnp.int32, (slots, pairs), 0) + plane * slots
    taken = slot == slot_of
    table_lane = lax.broadcasted_iota(jnp.int32, (slots, LANES), 1)
    entries = jnp.zeros((slots, LANES), jnp.int32)
    for at, value in enumerate(lines_of):
        listed = empty + jnp.sum(jnp.where(taken, value - empty, 0), axis=1, keepdims=True)
        entries = jnp.where(table_lane == at, listed, entries)
    table[...] = jnp.clip(entries, 0, empty)
    index_copy = pltpu.make_async_copy(table, index, small_sem.at[3])
    index_copy.start()
    for unit in units:
        unit[empty:, :] = jnp.zeros((TILE, LANES), jnp.float32)

    def forward(chunk):
        for step in (1, 2, 3):
            for upper in range(2):
                plane_arrival(step, upper, chunk).wait_recv()

                @pl.when(relays[upper])
                def _():
                    which = spot ^ step
                    relay_copy(
                        upper, chunk, which, place(upper, chunk, own_slot(upper, which))
                    ).start()

    def height_onward(source, up):
        origin = lax.div(source, look_rows) * 2 + lax.rem(spot, 2)
        if up:
            return (plane == planes - 2) & (origin < planes - 2)
        return (plane == 1) & (origin > 1)

    def height_relay(source, up):
        return pltpu.make_async_remote_copy(
            src_ref=heights.at[source],
            dst_ref=heights.at[source],
            send_sem=height_relay_send.at[up, source],
            recv_sem=height_recv.at[source],
            device_id={"date": me + BAND * (2 * up - 1)},
        )

    def height_pass():
        @pl.loop(0, planes)
        def _(source):
            for up in range(2):
                @pl.when(height_onward(source, up))
                def _():
                    height_arrival(source).wait_recv()
                    height_relay(source, up).start()

    own_rows = lax.broadcasted_iota(jnp.int32, (dates, LANES), 0) < BAND

    def compute(chunk):
        for upper in range(2):
            own_copy(upper, chunk).wait()

            @pl.when(gets_relays[upper])
            def _():
                relay_all(upper, chunk).wait_recv()

        start, width = chunks[chunk]

        @pl.loop(start, start + width)
        def _(block):
            phase = lax.div(block, steps)
            tile = lax.div(phase, HALVES)
            column = pl.multiple_of(lax.rem(block, steps * HALVES) * LANES, LANES)
            totals = []
            for look_row in range(look_rows):
                found = [None] * QUANTITIES

                def add(at, value):
                    found[at] = value if found[at] is None else found[at] + value

                for row in range(LOOK_ROWS):
                    flat = []
                    for upper in range(2):
                        source = (upper * tiles + tile) * look_rows + look_row
                        level = heights[source, row:row + 1, pl.ds(column, LANES)]
                        cosine, sine = cos_sin(scales[upper] * level)
                        at = pl.ds(look_row * LOOK_ROWS + row, dates, stride=TILE)
                        real = window[upper, 0, block, at, :]
                        imag = window[upper, 1, block, at, :]
                        flat.append((real * cosine - imag * sine, real * sine + imag * cosine))
                    own_real, own_imag = (jnp.where(own_rows, u, l) for l, u in zip(*flat))
                    add(0, own_real * own_real + own_imag * own_imag)
                    rest_real, rest_imag = (jnp.where(own_rows, l, u) for l, u in zip(*flat))
                    add(QUANTITIES - 1, rest_real * rest_real + rest_imag * rest_imag)
                    for distance in range(1, BAND + 1):
                        other_real, other_imag = (
                            jnp.where(
                                own_rows, pltpu.roll(u, dates - distance, 0), pltpu.roll(l, distance, 0)
                            )
                            for l, u in zip(*flat)
                        )
                        add(distance, own_real * other_real + own_imag * other_imag)
                        add(BAND + distance, own_imag * other_real - own_real * other_imag)
                totals.append(jnp.concatenate(found, axis=0))
            weights = box[
                pl.ds(pl.multiple_of(lax.rem(block, steps) * look_rows * LANES, LANES), look_rows * LANES), :
            ]
            summed = sums[phase]
            for piece in split(jnp.concatenate(totals, axis=1), 2):
                summed = summed + jnp.dot(piece, weights, preferred_element_type=jnp.float32)
            sums[phase] = summed

    line = lax.broadcasted_iota(jnp.int32, (LINES, LANES), 0)
    turned = (line >= (1 + BAND) * TILE) & (line < (1 + 2 * BAND) * TILE) & ((line & BAND) == BAND)
    scale = jnp.where(turned, -1.0, 1.0) * (1.0 / (LOOK_ROWS * LOOK_COLS))

    def unit_lines(phase, which):
        return units[phase].at[pl.ds(pl.multiple_of(which * UNIT, TILE), UNIT), :]

    def unit_copy(phase, to_plane):
        return pltpu.make_async_remote_copy(
            src_ref=unit_lines(phase, plane),
            dst_ref=unit_lines(phase, plane),
            send_sem=unit_send.at[phase, to_plane],
            recv_sem=unit_recv.at[phase, plane],
            device_id={"date": to_plane * BAND + spot},
        )

    def unit_arrival(phase, source):
        return pltpu.make_async_remote_copy(
            src_ref=unit_lines(phase, source),
            dst_ref=unit_lines(phase, source),
            send_sem=unit_send.at[phase, source],
            recv_sem=unit_recv.at[phase, source],
            device_id={"date": source * BAND + spot},
        )

    def other_plane(turn):
        return lax.rem(plane + turn, planes)

    def unit_start(phase):
        units[phase][pl.ds(pl.multiple_of(plane * UNIT, TILE), UNIT), :] = sums[phase, :UNIT] * scale[:UNIT]

        @pl.loop(1, planes)
        def _(turn):
            unit_copy(phase, other_plane(turn)).start()

    def ratio_of(near, far_side, first_power, second_power):
        squares = [v * v for v in (near, far_side)]
        squares = [v + pltpu.roll(v, CAP, 0) for v in squares]
        level = jnp.sqrt(jnp.where(own_rows, squares[0], squares[1]))
        return level / jnp.sqrt((first_power + EPSILON) * (second_power + EPSILON))

    def parcel(to):
        return pl.ds(pl.multiple_of(to * 3 * TILE, TILE), 3 * TILE)

    def slot_copy(phase, to):
        return pltpu.make_async_remote_copy(
            src_ref=outboxes[phase].at[parcel(to), :],
            dst_ref=plane_inbox.at[phase, spot],
            send_sem=slot_send.at[phase, to],
            recv_sem=slot_recv.at[phase, spot],
            device_id={"date": plane * BAND + to},
        )

    def slot_arrival(phase, source):
        return pltpu.make_async_remote_copy(
            src_ref=outboxes[phase].at[parcel(source), :],
            dst_ref=plane_inbox.at[phase, source],
            send_sem=slot_send.at[phase, source],
            recv_sem=slot_recv.at[phase, source],
            device_id={"date": plane * BAND + source},
        )

    def choose(phase):
        unit = units[phase]
        for which in range(BAND):
            for at in range(CAP):
                for part in range(PARTS):
                    line = jnp.clip(index[which * CAP + at, part], 0, planes * UNIT)
                    row = (which * 4 + part // 2) * TILE + part % 2 * CAP + at
                    staged[phase, row:row + 1, :] = unit[pl.ds(line, 1), :]
        for which in range(BAND):
            near, far_side, first_power, second_power = (
                staged[phase, (which * 4 + at) * TILE:(which * 4 + at + 1) * TILE, :] for at in range(4)
            )
            ratio = ratio_of(near, far_side, first_power, second_power)
            outboxes[phase][which * 3 * TILE:(which + 1) * 3 * TILE, :] = jnp.concatenate(
                [near, far_side, ratio], axis=0
            )
        for step in (2, 3, 1):
            slot_copy(phase, spot ^ step).start()
        plane_inbox[phase, spot] = outboxes[phase][parcel(spot), :]

    index_copy.wait()

    last = len(chunks) - 1
    computed = 0
    for chunk in range(len(chunks) + LAG):
        if chunk <= last:
            forward(chunk)
        if chunk == 0:
            height_pass()
        while computed <= min(chunk - LAG, last):
            if computed == 0:
                @pl.loop(0, planes)
                def _(source):
                    @pl.when(jnp.logical_not(height_onward(source, 0) | height_onward(source, 1)))
                    def _():
                        height_arrival(source).wait_recv()

            compute(computed)
            start, width = chunks[computed]
            if (start + width) % steps == 0 and computed < last:
                unit_start(start // steps)
            computed += 1

    size = len(places) * CAP
    for at, piece in enumerate(split(sums[early] * scale, PIECES)):
        stack[at * LINES:(at + 1) * LINES, :] = piece
    chosen[...] = jnp.dot(picks[...], stack[...], preferred_element_type=jnp.float32)

    def peer(step):
        return lax.rem(me + step, devices)

    def out_copy(to):
        return pltpu.make_async_remote_copy(
            src_ref=outbox.at[to],
            dst_ref=inbox.at[me],
            send_sem=out_send.at[to],
            recv_sem=out_recv.at[me],
            device_id={"date": to},
        )

    def out_arrival(source):
        return pltpu.make_async_remote_copy(
            src_ref=outbox.at[source],
            dst_ref=inbox.at[source],
            send_sem=out_send.at[source],
            recv_sem=out_recv.at[source],
            device_id={"date": source},
        )

    @pl.loop(0, devices // BAND)
    def _(some):
        for one in range(BAND):
            which = lax.rem(plane + some, planes) * BAND + one
            near, far_side, first_power, second_power = (
                chosen[pl.ds(pl.multiple_of(which * size + at * TILE, TILE), TILE), :] for at in range(4)
            )
            for at, value in enumerate((near, far_side, ratio_of(near, far_side, first_power, second_power))):
                outbox[which, at] = value

        for one in range(BAND):
            to = lax.rem(plane + some, planes) * BAND + one

            @pl.when(to != me)
            def _():
                out_copy(to).start()


    inbox[me] = outbox[me]

    for phase in range(early):
        @pl.loop(1, planes)
        def _(turn):
            unit_arrival(phase, other_plane(turn)).wait_recv()

        choose(phase)

    @pl.loop(0, planes)
    def _(to_plane):
        @pl.when(height_direct(to_plane))
        def _():
            height_copy(to_plane).wait_send()

    @pl.loop(0, planes)
    def _(source):
        for up in range(2):
            @pl.when(height_onward(source, up))
            def _():
                height_relay(source, up).wait_send()

    for chunk in range(len(chunks)):
        for upper in range(2):
            plane_all(upper, chunk).wait_send()

            @pl.when(relays[upper])
            def _():
                relay_all(upper, chunk).wait_send()

    for phase in range(early):
        for step in range(1, BAND):
            slot_arrival(phase, spot ^ step).wait_recv()

    @pl.loop(1, devices)
    def _(step):
        out_arrival(peer(step)).wait_recv()

    for phase in range(early):
        @pl.loop(1, planes)
        def _(turn):
            unit_copy(phase, other_plane(turn)).wait_send()

        for step in range(1, BAND):
            slot_copy(phase, spot ^ step).wait_send()

    @pl.loop(1, devices)
    def _(step):
        out_copy(peer(step)).wait_send()


def assemble(planes, phases, inbox, plane_inbox, looks_out, coherence_out):
    tiles = phases // HALVES
    early = phases - 1
    part_lanes = LANES // HALVES
    look_rows = TILE // LOOK_ROWS
    looks = coherence_out.shape[0] // CAP
    left = lax.broadcasted_iota(jnp.int32, (TILE, LANES), 1) < part_lanes
    for quarter in range(BAND):
        for tile in range(tiles):
            for part in range(3):
                sides = []
                for half in range(HALVES):
                    phase = tile * HALVES + half
                    if phase < early:
                        sides.append(plane_inbox[phase, quarter, part * TILE:(part + 1) * TILE, :])
                    else:
                        value = inbox[quarter, part]
                        for other in range(1, planes):
                            value = value + inbox[other * BAND + quarter, part]
                        sides.append(value)
                here, there = sides
                values = (
                    jnp.where(left, here, pltpu.roll(there, part_lanes, 1)),
                    jnp.where(left, pltpu.roll(here, part_lanes, 1), there),
                )
                for look_row, value in enumerate(values):
                    for c in range(2):
                        upper = 1 - part if part < 2 else 1 - c
                        at = tile_of(tiles, quarter, upper, tile) * look_rows + look_row
                        piece = value[c * CAP:(c + 1) * CAP]
                        if part < 2:
                            looks_out[pl.ds(c * looks + at, CAP, stride=2 * looks), :] = piece
                        else:
                            coherence_out[pl.ds(at, CAP, stride=looks), :] = piece


def body(images, height_phase, baseline, pair_list, pair_owner):
    devices = lax.axis_size("date")
    rows, columns = images.shape[2:]
    lanes = columns // LOOK_COLS
    looks = rows // LOOK_ROWS
    planes = devices // BAND
    tiles = rows // (2 * BAND * TILE)
    phases = tiles * HALVES
    early = phases - 1
    blocks = columns // (HALVES * LANES)
    chunks = len(chunk_list(phases, blocks))
    dates = 2 * BAND
    pairs = pair_list.shape[0]
    assert lanes == LANES and rows == LOOK_ROWS * devices and TILE == 2 * LOOK_ROWS and HALVES == 2
    assert rows % (2 * BAND * TILE) == 0 and columns % (HALVES * LANES) == 0 and blocks > 5
    assert PIECES * LINES <= DEPTH
    vmem = pl.BlockSpec(memory_space=pltpu.VMEM)
    hbm = pl.BlockSpec(memory_space=pltpu.HBM)
    dma = pltpu.SemaphoreType.DMA
    tiled = images[0].reshape(2, rows // TILE, TILE, columns // LANES, LANES).transpose(0, 1, 3, 2, 4)
    inputs = [
        pltpu.with_memory_space_constraint(v, pltpu.HBM)
        for v in (tiled, height_phase, baseline[None], pair_list.T, pair_owner.T)
    ]
    scratch = [
        pltpu.VMEM((2, 2, phases * blocks, dates * TILE, LANES), jnp.float32),
        pltpu.VMEM((planes, LOOK_ROWS, columns), jnp.float32),
        pltpu.VMEM((2 * columns // HALVES, lanes), jnp.bfloat16),
        pltpu.VMEM((phases, LINES, lanes), jnp.float32),
        pltpu.VMEM((devices * TILE * CAP, DEPTH), jnp.bfloat16),
        pltpu.VMEM((DEPTH, lanes), jnp.bfloat16),
        pltpu.VMEM((devices * TILE * CAP, lanes), jnp.float32),
        pltpu.VMEM((devices, 3, TILE, lanes), jnp.float32),
        pltpu.VMEM((1, devices), jnp.float32),
        pltpu.VMEM((2, pairs), jnp.int32),
        pltpu.VMEM((1, pairs), jnp.int32),
        pltpu.VMEM((BAND * CAP, LANES), jnp.int32),
        pltpu.SMEM((BAND * CAP, LANES), jnp.int32),
        pltpu.VMEM((early, BAND * 4 * TILE, lanes), jnp.float32),
    ]
    scratch += [pltpu.VMEM((planes * UNIT + TILE, lanes), jnp.float32)] * early
    scratch += [pltpu.VMEM((BAND * 3 * TILE, lanes), jnp.float32)] * early
    size = sum(math.prod(s.shape) * jnp.dtype(s.dtype).itemsize for s in scratch)
    scratch += [
        pltpu.SemaphoreType.REGULAR((planes - 1,)),
        dma((4,)),
        dma((2, chunks)),
        dma((2, chunks)),
        dma((2, chunks, BAND)),
        dma((2, chunks)),
        dma((planes,)),
        dma((planes,)),
        dma((2, planes)),
        dma((early, planes)),
        dma((early, planes)),
        dma((early, BAND)),
        dma((early, BAND)),
        dma((devices,)),
        dma((devices,)),
    ]
    arrived = pl.pallas_call(
        functools.partial(kernel, devices, phases),
        out_shape=(
            jax.ShapeDtypeStruct((devices, 3, TILE, lanes), jnp.float32),
            jax.ShapeDtypeStruct((early, BAND, 3 * TILE, lanes), jnp.float32),
        ),
        in_specs=[hbm] * 5,
        out_specs=(vmem, vmem),
        scratch_shapes=scratch,
        compiler_params=pltpu.CompilerParams(
            collective_id=0, has_side_effects=True, vmem_limit_bytes=size + (6 << 20)
        ),
    )(*inputs)
    look, coherence = pl.pallas_call(
        functools.partial(assemble, planes, phases),
        out_shape=(
            jax.ShapeDtypeStruct((CAP * 2 * looks, lanes), jnp.float32),
            jax.ShapeDtypeStruct((CAP * looks, lanes), jnp.float32),
        ),
        in_specs=[vmem, vmem],
        out_specs=(vmem, vmem),
        compiler_params=pltpu.CompilerParams(vmem_limit_bytes=8 << 20),
    )(*arrived)
    return look.reshape(CAP, 2, looks, lanes), coherence.reshape(CAP, looks, lanes)


def solution(mesh):
    in_specs = (
        P(("groups", "date"), None, None, None),
        P(("groups", "date"), None),
        P("groups"),
        P(),
        P(),
    )
    out_specs = (P(("groups", "date"), None, None, None), P(("groups", "date"), None, None))
    return jax.shard_map(body, mesh=mesh, in_specs=in_specs, out_specs=out_specs, check_vma=False)
```

```python
import functools
import math

import jax
import jax.numpy as jnp
from jax import lax
from jax.experimental import pallas as pl
from jax.experimental.pallas import tpu as pltpu
from jax.sharding import PartitionSpec as P

LOOK_ROWS = 4
LOOK_COLS = 20
CAP = 4
BAND = 4
EPSILON = 1e-06
LANES = 128
TILE = 8
HALVES = 2
QUANTITIES = 2 + 2 * BAND
LINES = QUANTITIES * TILE
UNIT = LINES - TILE
PARTS = 8
PIECES = 3
DEPTH = 256
FIRST = 2
LAG = 3


def split(values, parts):
    pieces = []
    for _ in range(parts):
        piece = values.astype(jnp.bfloat16)
        pieces.append(piece)
        values = values - piece.astype(jnp.float32)
    return pieces


def horner(square, terms):
    value = square * terms[-1] + terms[-2]
    for term in terms[-3::-1]:
        value = value * square + term
    return value


COSINE = (1, -0.5, 0.041666653, -0.00138887553, 2.47949283e-05, -2.73862867e-07, 1.86794624e-09)
SINE = (1, -0.166666627, 0.00833326671, -0.000198363021, 2.73895216e-06, -2.24168115e-08)


def cos_sin(angle):
    square = angle * angle
    return horner(square, COSINE), horner(square, SINE) * angle


def chunk_list(phases, blocks):
    chunks = []
    for phase in range(phases):
        widths = [blocks - blocks // 2, blocks // 2] if phase < phases - 1 else [blocks - 5, 3, 2]
        start = phase * blocks
        for width in widths:
            chunks.append((start, width))
            start += width
    return chunks


def tile_of(tiles, quarter, upper, tile):
    return (quarter >> 1) + 2 * ((quarter & 1) + 2 * (upper * tiles + tile))


def kernel(
    devices, phases, images, height, baseline_in, pair_list_in, pair_owner_in, inbox, plane_inbox,
    window, heights, box, sums, picks, stack, chosen, outbox, baseline, pair_list, pair_owner,
    table, index, staged, *rest,
):
    early = phases - 1
    units, outboxes = rest[:early], rest[early:2 * early]
    (
        far, small_sem, plane_send, relay_send, plane_recv, relay_recv, height_send, height_recv, height_relay_send,
        unit_send, unit_recv, slot_send, slot_recv, out_send, out_recv,
    ) = rest[2 * early:]
    me = lax.axis_index("date")
    planes = devices // BAND
    plane = lax.div(me, BAND)
    spot = lax.rem(me, BAND)
    tiles = phases // HALVES
    column_tiles = images.shape[2]
    columns = column_tiles * LANES
    part_columns = columns // HALVES
    steps = part_columns // LANES
    chunks = chunk_list(phases, steps)
    side = BAND * TILE
    dates = 2 * BAND
    part_lanes = LANES // HALVES
    look_rows = TILE // LOOK_ROWS
    below, above = plane > 0, plane < planes - 1

    barrier = pltpu.get_barrier_semaphore()

    def hello(to):
        pl.semaphore_signal(barrier, inc=1, device_id={"date": to})

    for step in range(1, BAND):
        hello(plane * BAND + (spot ^ step))

    @pl.when(below)
    def _():
        hello(me - BAND)

    @pl.when(above)
    def _():
        hello(me + BAND)

    reader = spot - lax.rem(spot, look_rows) + lax.rem(plane, 2)
    own_height = lax.div(plane, 2) * look_rows + lax.rem(spot, look_rows)

    def small_copies():
        return [
            pltpu.make_async_copy(source, to, small_sem.at[at])
            for at, (source, to) in enumerate(
                ((baseline_in, baseline), (pair_list_in, pair_list), (pair_owner_in, pair_owner))
            )
        ]

    def height_copy(to_plane):
        return pltpu.make_async_remote_copy(
            src_ref=height,
            dst_ref=heights.at[own_height],
            send_sem=height_send.at[to_plane],
            recv_sem=height_recv.at[own_height],
            device_id={"date": to_plane * BAND + reader},
        )

    def height_own():
        return pltpu.make_async_copy(height, heights.at[own_height], height_recv.at[own_height])

    def height_arrival(source):
        return pltpu.make_async_remote_copy(
            src_ref=height,
            dst_ref=heights.at[source],
            send_sem=height_send.at[0],
            recv_sem=height_recv.at[source],
            device_id={"date": me},
        )

    def lines(quarter, upper, chunk):
        start, width = chunks[chunk]
        tile = tile_of(tiles, quarter, upper, start // (steps * HALVES))
        return images.at[:, tile, start % (steps * HALVES):start % (steps * HALVES) + width]

    def place(upper, chunk, slot, size=TILE):
        start, width = chunks[chunk]
        return window.at[upper, :, start:start + width, pl.ds(pl.multiple_of(slot * TILE, TILE), size), :]

    def own_slot(upper, which):
        return (1 - upper) * BAND + which

    def plane_copy(step, upper, chunk):
        to = spot ^ step
        return pltpu.make_async_remote_copy(
            src_ref=lines(to, upper, chunk),
            dst_ref=place(upper, chunk, own_slot(upper, spot)),
            send_sem=plane_send.at[upper, chunk],
            recv_sem=plane_recv.at[upper, chunk, spot],
            device_id={"date": plane * BAND + to},
        )

    def plane_arrival(step, upper, chunk):
        source = spot ^ step
        return pltpu.make_async_remote_copy(
            src_ref=lines(source, upper, chunk),
            dst_ref=place(upper, chunk, own_slot(upper, source)),
            send_sem=plane_send.at[upper, chunk],
            recv_sem=plane_recv.at[upper, chunk, source],
            device_id={"date": plane * BAND + source},
        )

    def own_copy(upper, chunk):
        return pltpu.make_async_copy(
            lines(spot, upper, chunk),
            place(upper, chunk, own_slot(upper, spot)),
            plane_recv.at[upper, chunk, spot],
        )

    relays = (above, below)
    gets_relays = (below, above)

    def relay_copy(upper, chunk, which, source):
        return pltpu.make_async_remote_copy(
            src_ref=source,
            dst_ref=place(upper, chunk, upper * BAND + which),
            send_sem=relay_send.at[upper, chunk],
            recv_sem=relay_recv.at[upper, chunk],
            device_id={"date": me + BAND * (1 - 2 * upper)},
        )

    def relay_all(upper, chunk):
        return pltpu.make_async_remote_copy(
            src_ref=place(upper, chunk, (1 - upper) * BAND, side),
            dst_ref=place(upper, chunk, upper * BAND, side),
            send_sem=relay_send.at[upper, chunk],
            recv_sem=relay_recv.at[upper, chunk],
            device_id={"date": me},
        )

    def plane_all(upper, chunk):
        return pltpu.make_async_remote_copy(
            src_ref=place(upper, chunk, 0, side - TILE),
            dst_ref=place(upper, chunk, 0, side - TILE),
            send_sem=plane_send.at[upper, chunk],
            recv_sem=relay_recv.at[upper, chunk],
            device_id={"date": me},
        )

    def own_relays(chunk):
        for upper in range(2):
            @pl.when(relays[upper])
            def _():
                relay_copy(upper, chunk, spot, lines(spot, upper, chunk)).start()

    for copy in small_copies():
        copy.start()
    pl.semaphore_wait(barrier, BAND - 1 + jnp.where(below, 1, 0) + jnp.where(above, 1, 0))

    def rows_out(chunk):
        for step in (2, 3, 1):
            for upper in range(2):
                plane_copy(step, upper, chunk).start()
        for upper in range(2):
            own_copy(upper, chunk).start()

    for chunk in range(FIRST):
        rows_out(chunk)

    def height_direct(to_plane):
        return (to_plane * BAND + reader != me) & (
            height_near(to_plane) | ((to_plane > 0) & (to_plane < planes - 1))
        )

    def height_near(to_plane):
        return (to_plane - plane < 2) & (plane - to_plane < 2)

    def meet(turn):
        @pl.when(below)
        def _():
            pl.semaphore_signal(far.at[turn], inc=1, device_id={"date": me - BAND})

        @pl.when(above)
        def _():
            pl.semaphore_signal(far.at[turn], inc=1, device_id={"date": me + BAND})

        pl.semaphore_wait(far.at[turn], jnp.where(below, 1, 0) + jnp.where(above, 1, 0))

    @pl.when(reader == spot)
    def _():
        height_own().start()

    meet(0)

    @pl.loop(0, planes)
    def _(to_plane):
        @pl.when(height_direct(to_plane) & height_near(to_plane))
        def _():
            height_copy(to_plane).start()

    for chunk in range(len(chunks)):
        own_relays(chunk)

    for turn in range(1, planes - 1):
        meet(turn)

    @pl.loop(0, planes)
    def _(to_plane):
        @pl.when(height_direct(to_plane) & jnp.logical_not(height_near(to_plane)))
        def _():
            height_copy(to_plane).start()

    for chunk in range(FIRST, len(chunks)):
        rows_out(chunk)

    for upper in range(2):
        @pl.when(jnp.logical_not(gets_relays[upper]))
        def _():
            @pl.loop(0, phases * steps)
            def _(block):
                window[upper, :, block, upper * side:(upper + 1) * side, :] = jnp.zeros(
                    (2, side, LANES), jnp.float32
                )

    @pl.loop(0, steps)
    def _(block):
        shape = (look_rows * LANES, LANES)
        line = lax.broadcasted_iota(jnp.int32, shape, 0)
        position = block * LANES + (line & (LANES - 1))
        target = lax.broadcasted_iota(jnp.int32, shape, 1) - jnp.where(line >= LANES, part_lanes, 0)
        target = target * LOOK_COLS
        box[pl.ds(pl.multiple_of(block * look_rows * LANES, look_rows * LANES), look_rows * LANES), :] = jnp.where(
            (position >= target) & (position < target + LOOK_COLS), 1.0, 0.0
        ).astype(jnp.bfloat16)

    sums[...] = jnp.zeros_like(sums)
    stack[...] = jnp.zeros_like(stack)

    for copy in small_copies():
        copy.wait()

    lane = lax.broadcasted_iota(jnp.int32, (dates, devices), 1)
    date = lax.broadcasted_iota(jnp.int32, (dates, devices), 0)
    scales = []
    for upper in range(2):
        chosen_date = lane == date + (plane - 1 + upper) * BAND
        scales.append(
            jnp.sum(jnp.where(chosen_date, baseline[...], 0.0), axis=1, keepdims=True)
        )

    owner = pair_owner[...]
    pairs = owner.shape[1]
    down = lax.broadcasted_iota(jnp.int32, (pairs, pairs), 0)
    across = lax.broadcasted_iota(jnp.int32, (pairs, pairs), 1)
    owner_column = jnp.sum(jnp.where(down == across, owner, 0), axis=1, keepdims=True)
    earlier = (owner_column == owner) & (down < across)
    slot_of = owner * CAP + jnp.sum(jnp.where(earlier, 1, 0), axis=0, keepdims=True)
    first, second = pair_list[0:1, :], pair_list[1:2, :]
    distance = second - first
    first_here = lax.div(first, BAND) == plane
    second_here = lax.div(second, BAND) == plane
    first_at = lax.rem(first, BAND)
    second_at = lax.rem(second, BAND)
    others = (QUANTITIES - 1) * TILE
    places = (
        (first_here, first_at + distance * TILE),
        (first_here, first_at + (BAND + distance) * TILE),
        (second_here, second_at + distance * TILE + BAND),
        (second_here, second_at + (BAND + distance) * TILE + BAND),
        (first_here, first_at),
        (second_here, jnp.where(first_here, first_at + BAND, others + first_at)),
        (first_here, jnp.where(second_here, second_at, others + second_at + BAND)),
        (second_here, second_at + BAND),
    )
    total = devices * len(places) * CAP
    line = lax.broadcasted_iota(jnp.int32, (total, pairs), 0)
    part = (line & (len(places) * CAP - 1)) - (line & (CAP - 1))
    taken = lax.div(line, len(places)) - lax.div(line & (len(places) * CAP - 1), len(places)) + (line & (CAP - 1)) == slot_of
    listed = jnp.full((total, pairs), -1, jnp.int32)
    for at, (valid, value) in enumerate(places):
        listed = jnp.where(taken & valid & (part == at * CAP), value, listed)
    listed = jnp.max(listed.astype(jnp.float32), axis=1, keepdims=True)
    depth = lax.broadcasted_iota(jnp.int32, (total, DEPTH), 1).astype(jnp.float32)
    hit = (depth == listed)
    for piece in range(1, PIECES):
        hit = hit | (depth == listed + piece * LINES)
    picks[...] = jnp.where(hit & (listed >= 0.0), 1.0, 0.0).astype(jnp.bfloat16)

    first_line = lax.div(first, BAND) * UNIT + first_at
    second_line = lax.div(second, BAND) * UNIT + second_at
    lines_of = (
        first_line + distance * TILE,
        first_line + (BAND + distance) * TILE,
        second_line + distance * TILE + BAND,
        second_line + (BAND + distance) * TILE + BAND,
        first_line,
        first_line + BAND,
        second_line,
        second_line + BAND,
    )
    slots = BAND * CAP
    empty = planes * UNIT
    slot = lax.broadcasted_iota(jnp.int32, (slots, pairs), 0) + plane * slots
    taken = slot == slot_of
    table_lane = lax.broadcasted_iota(jnp.int32, (slots, LANES), 1)
    entries = jnp.zeros((slots, LANES), jnp.int32)
    for at, value in enumerate(lines_of):
        listed = empty + jnp.sum(jnp.where(taken, value - empty, 0), axis=1, keepdims=True)
        entries = jnp.where(table_lane == at, listed, entries)
    table[...] = jnp.clip(entries, 0, empty)
    index_copy = pltpu.make_async_copy(table, index, small_sem.at[3])
    index_copy.start()
    for unit in units:
        unit[empty:, :] = jnp.zeros((TILE, LANES), jnp.float32)

    def forward(chunk):
        for step in (1, 2, 3):
            for upper in range(2):
                plane_arrival(step, upper, chunk).wait_recv()

                @pl.when(relays[upper])
                def _():
                    which = spot ^ step
                    relay_copy(
                        upper, chunk, which, place(upper, chunk, own_slot(upper, which))
                    ).start()

    def height_onward(source, up):
        origin = lax.div(source, look_rows) * 2 + lax.rem(spot, 2)
        if up:
            return (plane == planes - 2) & (origin < planes - 2)
        return (plane == 1) & (origin > 1)

    def height_relay(source, up):
        return pltpu.make_async_remote_copy(
            src_ref=heights.at[source],
            dst_ref=heights.at[source],
            send_sem=height_relay_send.at[up, source],
            recv_sem=height_recv.at[source],
            device_id={"date": me + BAND * (2 * up - 1)},
        )

    def height_pass():
        @pl.loop(0, planes)
        def _(source):
            for up in range(2):
                @pl.when(height_onward(source, up))
                def _():
                    height_arrival(source).wait_recv()
                    height_relay(source, up).start()

    own_rows = lax.broadcasted_iota(jnp.int32, (dates, LANES), 0) < BAND

    def compute(chunk):
        for upper in range(2):
            own_copy(upper, chunk).wait()

            @pl.when(gets_relays[upper])
            def _():
                relay_all(upper, chunk).wait_recv()

        start, width = chunks[chunk]

        @pl.loop(start, start + width)
        def _(block):
            phase = lax.div(block, steps)
            tile = lax.div(phase, HALVES)
            column = pl.multiple_of(lax.rem(block, steps * HALVES) * LANES, LANES)
            totals = []
            for look_row in range(look_rows):
                found = [None] * QUANTITIES

                def add(at, value):
                    found[at] = value if found[at] is None else found[at] + value

                for row in range(LOOK_ROWS):
                    flat = []
                    for upper in range(2):
                        source = (upper * tiles + tile) * look_rows + look_row
                        level = heights[source, row:row + 1, pl.ds(column, LANES)]
                        cosine, sine = cos_sin(scales[upper] * level)
                        at = pl.ds(look_row * LOOK_ROWS + row, dates, stride=TILE)
                        real = window[upper, 0, block, at, :]
                        imag = window[upper, 1, block, at, :]
                        flat.append((real * cosine - imag * sine, real * sine + imag * cosine))
                    own_real, own_imag = (jnp.where(own_rows, u, l) for l, u in zip(*flat))
                    add(0, own_real * own_real + own_imag * own_imag)
                    rest_real, rest_imag = (jnp.where(own_rows, l, u) for l, u in zip(*flat))
                    add(QUANTITIES - 1, rest_real * rest_real + rest_imag * rest_imag)
                    for distance in range(1, BAND + 1):
                        other_real, other_imag = (
                            jnp.where(
                                own_rows, pltpu.roll(u, dates - distance, 0), pltpu.roll(l, distance, 0)
                            )
                            for l, u in zip(*flat)
                        )
                        add(distance, own_real * other_real + own_imag * other_imag)
                        add(BAND + distance, own_imag * other_real - own_real * other_imag)
                totals.append(jnp.concatenate(found, axis=0))
            weights = box[
                pl.ds(pl.multiple_of(lax.rem(block, steps) * look_rows * LANES, LANES), look_rows * LANES), :
            ]
            summed = sums[phase]
            for piece in split(jnp.concatenate(totals, axis=1), 2):
                summed = summed + jnp.dot(piece, weights, preferred_element_type=jnp.float32)
            sums[phase] = summed

    line = lax.broadcasted_iota(jnp.int32, (LINES, LANES), 0)
    turned = (line >= (1 + BAND) * TILE) & (line < (1 + 2 * BAND) * TILE) & ((line & BAND) == BAND)
    scale = jnp.where(turned, -1.0, 1.0) * (1.0 / (LOOK_ROWS * LOOK_COLS))

    def unit_lines(phase, which):
        return units[phase].at[pl.ds(pl.multiple_of(which * UNIT, TILE), UNIT), :]

    def unit_copy(phase, to_plane):
        return pltpu.make_async_remote_copy(
            src_ref=unit_lines(phase, plane),
            dst_ref=unit_lines(phase, plane),
            send_sem=unit_send.at[phase, to_plane],
            recv_sem=unit_recv.at[phase, plane],
            device_id={"date": to_plane * BAND + spot},
        )

    def unit_arrival(phase, source):
        return pltpu.make_async_remote_copy(
            src_ref=unit_lines(phase, source),
            dst_ref=unit_lines(phase, source),
            send_sem=unit_send.at[phase, source],
            recv_sem=unit_recv.at[phase, source],
            device_id={"date": source * BAND + spot},
        )

    def other_plane(turn):
        return lax.rem(plane + turn, planes)

    def unit_start(phase):
        units[phase][pl.ds(pl.multiple_of(plane * UNIT, TILE), UNIT), :] = sums[phase, :UNIT] * scale[:UNIT]

        @pl.loop(1, planes)
        def _(turn):
            unit_copy(phase, other_plane(turn)).start()

    def ratio_of(near, far_side, first_power, second_power):
        squares = [v * v for v in (near, far_side)]
        squares = [v + pltpu.roll(v, CAP, 0) for v in squares]
        level = jnp.sqrt(jnp.where(own_rows, squares[0], squares[1]))
        return level / jnp.sqrt((first_power + EPSILON) * (second_power + EPSILON))

    def parcel(to):
        return pl.ds(pl.multiple_of(to * 3 * TILE, TILE), 3 * TILE)

    def slot_copy(phase, to):
        return pltpu.make_async_remote_copy(
            src_ref=outboxes[phase].at[parcel(to), :],
            dst_ref=plane_inbox.at[phase, spot],
            send_sem=slot_send.at[phase, to],
            recv_sem=slot_recv.at[phase, spot],
            device_id={"date": plane * BAND + to},
        )

    def slot_arrival(phase, source):
        return pltpu.make_async_remote_copy(
            src_ref=outboxes[phase].at[parcel(source), :],
            dst_ref=plane_inbox.at[phase, source],
            send_sem=slot_send.at[phase, source],
            recv_sem=slot_recv.at[phase, source],
            device_id={"date": plane * BAND + source},
        )

    def choose(phase):
        unit = units[phase]
        for which in range(BAND):
            for at in range(CAP):
                for part in range(PARTS):
                    line = jnp.clip(index[which * CAP + at, part], 0, planes * UNIT)
                    row = (which * 4 + part // 2) * TILE + part % 2 * CAP + at
                    staged[phase, row:row + 1, :] = unit[pl.ds(line, 1), :]
        for which in range(BAND):
            near, far_side, first_power, second_power = (
                staged[phase, (which * 4 + at) * TILE:(which * 4 + at + 1) * TILE, :] for at in range(4)
            )
            ratio = ratio_of(near, far_side, first_power, second_power)
            outboxes[phase][which * 3 * TILE:(which + 1) * 3 * TILE, :] = jnp.concatenate(
                [near, far_side, ratio], axis=0
            )
        for step in (2, 3, 1):
            slot_copy(phase, spot ^ step).start()
        plane_inbox[phase, spot] = outboxes[phase][parcel(spot), :]

    index_copy.wait()

    last = len(chunks) - 1
    computed = 0
    for chunk in range(len(chunks) + LAG):
        if chunk <= last:
            forward(chunk)
        if chunk == 0:
            height_pass()
        while computed <= min(chunk - LAG, last):
            if computed == 0:
                @pl.loop(0, planes)
                def _(source):
                    @pl.when(jnp.logical_not(height_onward(source, 0) | height_onward(source, 1)))
                    def _():
                        height_arrival(source).wait_recv()

            compute(computed)
            start, width = chunks[computed]
            if (start + width) % steps == 0 and computed < last:
                unit_start(start // steps)
            computed += 1

    size = len(places) * CAP
    for at, piece in enumerate(split(sums[early] * scale, PIECES)):
        stack[at * LINES:(at + 1) * LINES, :] = piece
    chosen[...] = jnp.dot(picks[...], stack[...], preferred_element_type=jnp.float32)

    def peer(step):
        return lax.rem(me + step, devices)

    def out_copy(to):
        return pltpu.make_async_remote_copy(
            src_ref=outbox.at[to],
            dst_ref=inbox.at[me],
            send_sem=out_send.at[to],
            recv_sem=out_recv.at[me],
            device_id={"date": to},
        )

    def out_arrival(source):
        return pltpu.make_async_remote_copy(
            src_ref=outbox.at[source],
            dst_ref=inbox.at[source],
            send_sem=out_send.at[source],
            recv_sem=out_recv.at[source],
            device_id={"date": source},
        )

    @pl.loop(0, devices // BAND)
    def _(some):
        for one in range(BAND):
            which = lax.rem(plane + some, planes) * BAND + one
            near, far_side, first_power, second_power = (
                chosen[pl.ds(pl.multiple_of(which * size + at * TILE, TILE), TILE), :] for at in range(4)
            )
            for at, value in enumerate((near, far_side, ratio_of(near, far_side, first_power, second_power))):
                outbox[which, at] = value

        for one in range(BAND):
            to = lax.rem(plane + some, planes) * BAND + one

            @pl.when(to != me)
            def _():
                out_copy(to).start()


    inbox[me] = outbox[me]

    for phase in range(early):
        @pl.loop(1, planes)
        def _(turn):
            unit_arrival(phase, other_plane(turn)).wait_recv()

        choose(phase)

    @pl.loop(0, planes)
    def _(to_plane):
        @pl.when(height_direct(to_plane))
        def _():
            height_copy(to_plane).wait_send()

    @pl.loop(0, planes)
    def _(source):
        for up in range(2):
            @pl.when(height_onward(source, up))
            def _():
                height_relay(source, up).wait_send()

    for chunk in range(len(chunks)):
        for upper in range(2):
            plane_all(upper, chunk).wait_send()

            @pl.when(relays[upper])
            def _():
                relay_all(upper, chunk).wait_send()

    for phase in range(early):
        for step in range(1, BAND):
            slot_arrival(phase, spot ^ step).wait_recv()

    @pl.loop(1, devices)
    def _(step):
        out_arrival(peer(step)).wait_recv()

    for phase in range(early):
        @pl.loop(1, planes)
        def _(turn):
            unit_copy(phase, other_plane(turn)).wait_send()

        for step in range(1, BAND):
            slot_copy(phase, spot ^ step).wait_send()

    @pl.loop(1, devices)
    def _(step):
        out_copy(peer(step)).wait_send()


def assemble(planes, phases, inbox, plane_inbox, looks_out, coherence_out):
    tiles = phases // HALVES
    early = phases - 1
    part_lanes = LANES // HALVES
    look_rows = TILE // LOOK_ROWS
    looks = coherence_out.shape[0] // CAP
    left = lax.broadcasted_iota(jnp.int32, (TILE, LANES), 1) < part_lanes
    for quarter in range(BAND):
        for tile in range(tiles):
            for part in range(3):
                sides = []
                for half in range(HALVES):
                    phase = tile * HALVES + half
                    if phase < early:
                        sides.append(plane_inbox[phase, quarter, part * TILE:(part + 1) * TILE, :])
                    else:
                        value = inbox[quarter, part]
                        for other in range(1, planes):
                            value = value + inbox[other * BAND + quarter, part]
                        sides.append(value)
                here, there = sides
                values = (
                    jnp.where(left, here, pltpu.roll(there, part_lanes, 1)),
                    jnp.where(left, pltpu.roll(here, part_lanes, 1), there),
                )
                for look_row, value in enumerate(values):
                    for c in range(2):
                        upper = 1 - part if part < 2 else 1 - c
                        at = tile_of(tiles, quarter, upper, tile) * look_rows + look_row
                        piece = value[c * CAP:(c + 1) * CAP]
                        if part < 2:
                            looks_out[pl.ds(c * looks + at, CAP, stride=2 * looks), :] = piece
                        else:
                            coherence_out[pl.ds(at, CAP, stride=looks), :] = piece


def body(images, height_phase, baseline, pair_list, pair_owner):
    devices = lax.axis_size("date")
    rows, columns = images.shape[2:]
    lanes = columns // LOOK_COLS
    looks = rows // LOOK_ROWS
    planes = devices // BAND
    tiles = rows // (2 * BAND * TILE)
    phases = tiles * HALVES
    early = phases - 1
    blocks = columns // (HALVES * LANES)
    chunks = len(chunk_list(phases, blocks))
    dates = 2 * BAND
    pairs = pair_list.shape[0]
    assert lanes == LANES and rows == LOOK_ROWS * devices and TILE == 2 * LOOK_ROWS and HALVES == 2
    assert rows % (2 * BAND * TILE) == 0 and columns % (HALVES * LANES) == 0 and blocks > 5
    assert PIECES * LINES <= DEPTH
    vmem = pl.BlockSpec(memory_space=pltpu.VMEM)
    hbm = pl.BlockSpec(memory_space=pltpu.HBM)
    dma = pltpu.SemaphoreType.DMA
    tiled = images[0].reshape(2, rows // TILE, TILE, columns // LANES, LANES).transpose(0, 1, 3, 2, 4)
    inputs = [
        pltpu.with_memory_space_constraint(v, pltpu.HBM)
        for v in (tiled, height_phase, baseline[None], pair_list.T, pair_owner.T)
    ]
    scratch = [
        pltpu.VMEM((2, 2, phases * blocks, dates * TILE, LANES), jnp.float32),
        pltpu.VMEM((planes, LOOK_ROWS, columns), jnp.float32),
        pltpu.VMEM((2 * columns // HALVES, lanes), jnp.bfloat16),
        pltpu.VMEM((phases, LINES, lanes), jnp.float32),
        pltpu.VMEM((devices * TILE * CAP, DEPTH), jnp.bfloat16),
        pltpu.VMEM((DEPTH, lanes), jnp.bfloat16),
        pltpu.VMEM((devices * TILE * CAP, lanes), jnp.float32),
        pltpu.VMEM((devices, 3, TILE, lanes), jnp.float32),
        pltpu.VMEM((1, devices), jnp.float32),
        pltpu.VMEM((2, pairs), jnp.int32),
        pltpu.VMEM((1, pairs), jnp.int32),
        pltpu.VMEM((BAND * CAP, LANES), jnp.int32),
        pltpu.SMEM((BAND * CAP, LANES), jnp.int32),
        pltpu.VMEM((early, BAND * 4 * TILE, lanes), jnp.float32),
    ]
    scratch += [pltpu.VMEM((planes * UNIT + TILE, lanes), jnp.float32)] * early
    scratch += [pltpu.VMEM((BAND * 3 * TILE, lanes), jnp.float32)] * early
    size = sum(math.prod(s.shape) * jnp.dtype(s.dtype).itemsize for s in scratch)
    scratch += [
        pltpu.SemaphoreType.REGULAR((planes - 1,)),
        dma((4,)),
        dma((2, chunks)),
        dma((2, chunks)),
        dma((2, chunks, BAND)),
        dma((2, chunks)),
        dma((planes,)),
        dma((planes,)),
        dma((2, planes)),
        dma((early, planes)),
        dma((early, planes)),
        dma((early, BAND)),
        dma((early, BAND)),
        dma((devices,)),
        dma((devices,)),
    ]
    arrived = pl.pallas_call(
        functools.partial(kernel, devices, phases),
        out_shape=(
            jax.ShapeDtypeStruct((devices, 3, TILE, lanes), jnp.float32),
            jax.ShapeDtypeStruct((early, BAND, 3 * TILE, lanes), jnp.float32),
        ),
        in_specs=[hbm] * 5,
        out_specs=(vmem, vmem),
        scratch_shapes=scratch,
        compiler_params=pltpu.CompilerParams(
            collective_id=0, has_side_effects=True, vmem_limit_bytes=size + (6 << 20)
        ),
    )(*inputs)
    look, coherence = pl.pallas_call(
        functools.partial(assemble, planes, phases),
        out_shape=(
            jax.ShapeDtypeStruct((CAP * 2 * looks, lanes), jnp.float32),
            jax.ShapeDtypeStruct((CAP * looks, lanes), jnp.float32),
        ),
        in_specs=[vmem, vmem],
        out_specs=(vmem, vmem),
        compiler_params=pltpu.CompilerParams(vmem_limit_bytes=8 << 20),
    )(*arrived)
    return look.reshape(CAP, 2, looks, lanes), coherence.reshape(CAP, looks, lanes)


def solution(mesh):
    in_specs = (
        P(("groups", "date"), None, None, None),
        P(("groups", "date"), None),
        P("groups"),
        P(),
        P(),
    )
    out_specs = (P(("groups", "date"), None, None, None), P(("groups", "date"), None, None))
    return jax.shard_map(body, mesh=mesh, in_specs=in_specs, out_specs=out_specs, check_vma=False)
```

```python
import functools
import math

import jax
import jax.numpy as jnp
from jax import lax
from jax.experimental import pallas as pl
from jax.experimental.pallas import tpu as pltpu
from jax.sharding import PartitionSpec as P

LOOK_ROWS = 4
LOOK_COLS = 20
CAP = 4
BAND = 4
EPSILON = 1e-06
LANES = 128
TILE = 8
HALVES = 2
QUANTITIES = 2 + 2 * BAND
LINES = QUANTITIES * TILE
UNIT = LINES - TILE
PARTS = 8
PIECES = 3
DEPTH = 256
FIRST = 2
LAG = 3


def split(values, parts):
    pieces = []
    for _ in range(parts):
        piece = values.astype(jnp.bfloat16)
        pieces.append(piece)
        values = values - piece.astype(jnp.float32)
    return pieces


def horner(square, terms):
    value = square * terms[-1] + terms[-2]
    for term in terms[-3::-1]:
        value = value * square + term
    return value


COSINE = (1, -0.5, 0.041666653, -0.00138887553, 2.47949283e-05, -2.73862867e-07, 1.86794624e-09)
SINE = (1, -0.166666627, 0.00833326671, -0.000198363021, 2.73895216e-06, -2.24168115e-08)


def cos_sin(angle):
    square = angle * angle
    return horner(square, COSINE), horner(square, SINE) * angle


def chunk_list(phases, blocks):
    chunks = []
    for phase in range(phases):
        widths = [blocks - blocks // 2, blocks // 2] if phase < phases - 1 else [blocks - 6, 4, 2]
        start = phase * blocks
        for width in widths:
            chunks.append((start, width))
            start += width
    return chunks


def tile_of(tiles, quarter, upper, tile):
    return (quarter >> 1) + 2 * ((quarter & 1) + 2 * (upper * tiles + tile))


def kernel(
    devices, phases, images, height, baseline_in, pair_list_in, pair_owner_in, inbox, plane_inbox,
    window, heights, box, sums, picks, stack, chosen, outbox, baseline, pair_list, pair_owner,
    table, index, staged, *rest,
):
    early = phases - 1
    units, outboxes = rest[:early], rest[early:2 * early]
    (
        far, small_sem, plane_send, relay_send, plane_recv, relay_recv, height_send, height_recv, height_relay_send,
        unit_send, unit_recv, slot_send, slot_recv, out_send, out_recv,
    ) = rest[2 * early:]
    me = lax.axis_index("date")
    planes = devices // BAND
    plane = lax.div(me, BAND)
    spot = lax.rem(me, BAND)
    tiles = phases // HALVES
    column_tiles = images.shape[2]
    columns = column_tiles * LANES
    part_columns = columns // HALVES
    steps = part_columns // LANES
    chunks = chunk_list(phases, steps)
    side = BAND * TILE
    dates = 2 * BAND
    part_lanes = LANES // HALVES
    look_rows = TILE // LOOK_ROWS
    below, above = plane > 0, plane < planes - 1

    barrier = pltpu.get_barrier_semaphore()

    def hello(to):
        pl.semaphore_signal(barrier, inc=1, device_id={"date": to})

    for step in range(1, BAND):
        hello(plane * BAND + (spot ^ step))

    @pl.when(below)
    def _():
        hello(me - BAND)

    @pl.when(above)
    def _():
        hello(me + BAND)

    reader = spot - lax.rem(spot, look_rows) + lax.rem(plane, 2)
    own_height = lax.div(plane, 2) * look_rows + lax.rem(spot, look_rows)

    def small_copies():
        return [
            pltpu.make_async_copy(source, to, small_sem.at[at])
            for at, (source, to) in enumerate(
                ((baseline_in, baseline), (pair_list_in, pair_list), (pair_owner_in, pair_owner))
            )
        ]

    def height_copy(to_plane):
        return pltpu.make_async_remote_copy(
            src_ref=height,
            dst_ref=heights.at[own_height],
            send_sem=height_send.at[to_plane],
            recv_sem=height_recv.at[own_height],
            device_id={"date": to_plane * BAND + reader},
        )

    def height_own():
        return pltpu.make_async_copy(height, heights.at[own_height], height_recv.at[own_height])

    def height_arrival(source):
        return pltpu.make_async_remote_copy(
            src_ref=height,
            dst_ref=heights.at[source],
            send_sem=height_send.at[0],
            recv_sem=height_recv.at[source],
            device_id={"date": me},
        )

    def lines(quarter, upper, chunk):
        start, width = chunks[chunk]
        tile = tile_of(tiles, quarter, upper, start // (steps * HALVES))
        return images.at[:, tile, start % (steps * HALVES):start % (steps * HALVES) + width]

    def place(upper, chunk, slot, size=TILE):
        start, width = chunks[chunk]
        return window.at[upper, :, start:start + width, pl.ds(pl.multiple_of(slot * TILE, TILE), size), :]

    def own_slot(upper, which):
        return (1 - upper) * BAND + which

    def plane_copy(step, upper, chunk):
        to = spot ^ step
        return pltpu.make_async_remote_copy(
            src_ref=lines(to, upper, chunk),
            dst_ref=place(upper, chunk, own_slot(upper, spot)),
            send_sem=plane_send.at[upper, chunk],
            recv_sem=plane_recv.at[upper, chunk, spot],
            device_id={"date": plane * BAND + to},
        )

    def plane_arrival(step, upper, chunk):
        source = spot ^ step
        return pltpu.make_async_remote_copy(
            src_ref=lines(source, upper, chunk),
            dst_ref=place(upper, chunk, own_slot(upper, source)),
            send_sem=plane_send.at[upper, chunk],
            recv_sem=plane_recv.at[upper, chunk, source],
            device_id={"date": plane * BAND + source},
        )

    def own_copy(upper, chunk):
        return pltpu.make_async_copy(
            lines(spot, upper, chunk),
            place(upper, chunk, own_slot(upper, spot)),
            plane_recv.at[upper, chunk, spot],
        )

    relays = (above, below)
    gets_relays = (below, above)

    def relay_copy(upper, chunk, which, source):
        return pltpu.make_async_remote_copy(
            src_ref=source,
            dst_ref=place(upper, chunk, upper * BAND + which),
            send_sem=relay_send.at[upper, chunk],
            recv_sem=relay_recv.at[upper, chunk],
            device_id={"date": me + BAND * (1 - 2 * upper)},
        )

    def relay_all(upper, chunk):
        return pltpu.make_async_remote_copy(
            src_ref=place(upper, chunk, (1 - upper) * BAND, side),
            dst_ref=place(upper, chunk, upper * BAND, side),
            send_sem=relay_send.at[upper, chunk],
            recv_sem=relay_recv.at[upper, chunk],
            device_id={"date": me},
        )

    def plane_all(upper, chunk):
        return pltpu.make_async_remote_copy(
            src_ref=place(upper, chunk, 0, side - TILE),
            dst_ref=place(upper, chunk, 0, side - TILE),
            send_sem=plane_send.at[upper, chunk],
            recv_sem=relay_recv.at[upper, chunk],
            device_id={"date": me},
        )

    def own_relays(chunk):
        for upper in range(2):
            @pl.when(relays[upper])
            def _():
                relay_copy(upper, chunk, spot, lines(spot, upper, chunk)).start()

    for copy in small_copies():
        copy.start()
    pl.semaphore_wait(barrier, BAND - 1 + jnp.where(below, 1, 0) + jnp.where(above, 1, 0))

    def rows_out(chunk):
        for step in (2, 3, 1):
            for upper in range(2):
                plane_copy(step, upper, chunk).start()
        for upper in range(2):
            own_copy(upper, chunk).start()

    for chunk in range(FIRST):
        rows_out(chunk)

    def height_direct(to_plane):
        return (to_plane * BAND + reader != me) & (
            height_near(to_plane) | ((to_plane > 0) & (to_plane < planes - 1))
        )

    def height_near(to_plane):
        return (to_plane - plane < 2) & (plane - to_plane < 2)

    def meet(turn):
        @pl.when(below)
        def _():
            pl.semaphore_signal(far.at[turn], inc=1, device_id={"date": me - BAND})

        @pl.when(above)
        def _():
            pl.semaphore_signal(far.at[turn], inc=1, device_id={"date": me + BAND})

        pl.semaphore_wait(far.at[turn], jnp.where(below, 1, 0) + jnp.where(above, 1, 0))

    @pl.when(reader == spot)
    def _():
        height_own().start()

    meet(0)

    @pl.loop(0, planes)
    def _(to_plane):
        @pl.when(height_direct(to_plane) & height_near(to_plane))
        def _():
            height_copy(to_plane).start()

    for chunk in range(len(chunks)):
        own_relays(chunk)

    for turn in range(1, planes - 1):
        meet(turn)

    @pl.loop(0, planes)
    def _(to_plane):
        @pl.when(height_direct(to_plane) & jnp.logical_not(height_near(to_plane)))
        def _():
            height_copy(to_plane).start()

    for chunk in range(FIRST, len(chunks)):
        rows_out(chunk)

    for upper in range(2):
        @pl.when(jnp.logical_not(gets_relays[upper]))
        def _():
            @pl.loop(0, phases * steps)
            def _(block):
                window[upper, :, block, upper * side:(upper + 1) * side, :] = jnp.zeros(
                    (2, side, LANES), jnp.float32
                )

    @pl.loop(0, steps)
    def _(block):
        shape = (look_rows * LANES, LANES)
        line = lax.broadcasted_iota(jnp.int32, shape, 0)
        position = block * LANES + (line & (LANES - 1))
        target = lax.broadcasted_iota(jnp.int32, shape, 1) - jnp.where(line >= LANES, part_lanes, 0)
        target = target * LOOK_COLS
        box[pl.ds(pl.multiple_of(block * look_rows * LANES, look_rows * LANES), look_rows * LANES), :] = jnp.where(
            (position >= target) & (position < target + LOOK_COLS), 1.0, 0.0
        ).astype(jnp.bfloat16)

    sums[...] = jnp.zeros_like(sums)
    stack[...] = jnp.zeros_like(stack)

    for copy in small_copies():
        copy.wait()

    lane = lax.broadcasted_iota(jnp.int32, (dates, devices), 1)
    date = lax.broadcasted_iota(jnp.int32, (dates, devices), 0)
    scales = []
    for upper in range(2):
        chosen_date = lane == date + (plane - 1 + upper) * BAND
        scales.append(
            jnp.sum(jnp.where(chosen_date, baseline[...], 0.0), axis=1, keepdims=True)
        )

    owner = pair_owner[...]
    pairs = owner.shape[1]
    down = lax.broadcasted_iota(jnp.int32, (pairs, pairs), 0)
    across = lax.broadcasted_iota(jnp.int32, (pairs, pairs), 1)
    owner_column = jnp.sum(jnp.where(down == across, owner, 0), axis=1, keepdims=True)
    earlier = (owner_column == owner) & (down < across)
    slot_of = owner * CAP + jnp.sum(jnp.where(earlier, 1, 0), axis=0, keepdims=True)
    first, second = pair_list[0:1, :], pair_list[1:2, :]
    distance = second - first
    first_here = lax.div(first, BAND) == plane
    second_here = lax.div(second, BAND) == plane
    first_at = lax.rem(first, BAND)
    second_at = lax.rem(second, BAND)
    others = (QUANTITIES - 1) * TILE
    places = (
        (first_here, first_at + distance * TILE),
        (first_here, first_at + (BAND + distance) * TILE),
        (second_here, second_at + distance * TILE + BAND),
        (second_here, second_at + (BAND + distance) * TILE + BAND),
        (first_here, first_at),
        (second_here, jnp.where(first_here, first_at + BAND, others + first_at)),
        (first_here, jnp.where(second_here, second_at, others + second_at + BAND)),
        (second_here, second_at + BAND),
    )
    total = devices * len(places) * CAP
    line = lax.broadcasted_iota(jnp.int32, (total, pairs), 0)
    part = (line & (len(places) * CAP - 1)) - (line & (CAP - 1))
    taken = lax.div(line, len(places)) - lax.div(line & (len(places) * CAP - 1), len(places)) + (line & (CAP - 1)) == slot_of
    listed = jnp.full((total, pairs), -1, jnp.int32)
    for at, (valid, value) in enumerate(places):
        listed = jnp.where(taken & valid & (part == at * CAP), value, listed)
    listed = jnp.max(listed.astype(jnp.float32), axis=1, keepdims=True)
    depth = lax.broadcasted_iota(jnp.int32, (total, DEPTH), 1).astype(jnp.float32)
    hit = (depth == listed)
    for piece in range(1, PIECES):
        hit = hit | (depth == listed + piece * LINES)
    picks[...] = jnp.where(hit & (listed >= 0.0), 1.0, 0.0).astype(jnp.bfloat16)

    first_line = lax.div(first, BAND) * UNIT + first_at
    second_line = lax.div(second, BAND) * UNIT + second_at
    lines_of = (
        first_line + distance * TILE,
        first_line + (BAND + distance) * TILE,
        second_line + distance * TILE + BAND,
        second_line + (BAND + distance) * TILE + BAND,
        first_line,
        first_line + BAND,
        second_line,
        second_line + BAND,
    )
    slots = BAND * CAP
    empty = planes * UNIT
    slot = lax.broadcasted_iota(jnp.int32, (slots, pairs), 0) + plane * slots
    taken = slot == slot_of
    table_lane = lax.broadcasted_iota(jnp.int32, (slots, LANES), 1)
    entries = jnp.zeros((slots, LANES), jnp.int32)
    for at, value in enumerate(lines_of):
        listed = empty + jnp.sum(jnp.where(taken, value - empty, 0), axis=1, keepdims=True)
        entries = jnp.where(table_lane == at, listed, entries)
    table[...] = jnp.clip(entries, 0, empty)
    index_copy = pltpu.make_async_copy(table, index, small_sem.at[3])
    index_copy.start()
    for unit in units:
        unit[empty:, :] = jnp.zeros((TILE, LANES), jnp.float32)

    def forward(chunk):
        for step in (1, 2, 3):
            for upper in range(2):
                plane_arrival(step, upper, chunk).wait_recv()

                @pl.when(relays[upper])
                def _():
                    which = spot ^ step
                    relay_copy(
                        upper, chunk, which, place(upper, chunk, own_slot(upper, which))
                    ).start()

    def height_onward(source, up):
        origin = lax.div(source, look_rows) * 2 + lax.rem(spot, 2)
        if up:
            return (plane == planes - 2) & (origin < planes - 2)
        return (plane == 1) & (origin > 1)

    def height_relay(source, up):
        return pltpu.make_async_remote_copy(
            src_ref=heights.at[source],
            dst_ref=heights.at[source],
            send_sem=height_relay_send.at[up, source],
            recv_sem=height_recv.at[source],
            device_id={"date": me + BAND * (2 * up - 1)},
        )

    def height_pass():
        @pl.loop(0, planes)
        def _(source):
            for up in range(2):
                @pl.when(height_onward(source, up))
                def _():
                    height_arrival(source).wait_recv()
                    height_relay(source, up).start()

    own_rows = lax.broadcasted_iota(jnp.int32, (dates, LANES), 0) < BAND

    def compute(chunk):
        for upper in range(2):
            own_copy(upper, chunk).wait()

            @pl.when(gets_relays[upper])
            def _():
                relay_all(upper, chunk).wait_recv()

        start, width = chunks[chunk]

        @pl.loop(start, start + width, unroll=width == 2)
        def _(block):
            phase = lax.div(block, steps)
            tile = lax.div(phase, HALVES)
            column = pl.multiple_of(lax.rem(block, steps * HALVES) * LANES, LANES)
            totals = []
            for look_row in range(look_rows):
                found = [None] * QUANTITIES

                def add(at, value):
                    found[at] = value if found[at] is None else found[at] + value

                for row in range(LOOK_ROWS):
                    flat = []
                    for upper in range(2):
                        source = (upper * tiles + tile) * look_rows + look_row
                        level = heights[source, row:row + 1, pl.ds(column, LANES)]
                        cosine, sine = cos_sin(scales[upper] * level)
                        at = pl.ds(look_row * LOOK_ROWS + row, dates, stride=TILE)
                        real = window[upper, 0, block, at, :]
                        imag = window[upper, 1, block, at, :]
                        flat.append((real * cosine - imag * sine, real * sine + imag * cosine))
                    own_real, own_imag = (jnp.where(own_rows, u, l) for l, u in zip(*flat))
                    add(0, own_real * own_real + own_imag * own_imag)
                    rest_real, rest_imag = (jnp.where(own_rows, l, u) for l, u in zip(*flat))
                    add(QUANTITIES - 1, rest_real * rest_real + rest_imag * rest_imag)
                    for distance in range(1, BAND + 1):
                        other_real, other_imag = (
                            jnp.where(
                                own_rows, pltpu.roll(u, dates - distance, 0), pltpu.roll(l, distance, 0)
                            )
                            for l, u in zip(*flat)
                        )
                        add(distance, own_real * other_real + own_imag * other_imag)
                        add(BAND + distance, own_imag * other_real - own_real * other_imag)
                totals.append(jnp.concatenate(found, axis=0))
            weights = box[
                pl.ds(pl.multiple_of(lax.rem(block, steps) * look_rows * LANES, LANES), look_rows * LANES), :
            ]
            summed = sums[phase]
            for piece in split(jnp.concatenate(totals, axis=1), 2):
                summed = summed + jnp.dot(piece, weights, preferred_element_type=jnp.float32)
            sums[phase] = summed

    line = lax.broadcasted_iota(jnp.int32, (LINES, LANES), 0)
    turned = (line >= (1 + BAND) * TILE) & (line < (1 + 2 * BAND) * TILE) & ((line & BAND) == BAND)
    scale = jnp.where(turned, -1.0, 1.0) * (1.0 / (LOOK_ROWS * LOOK_COLS))

    def unit_lines(phase, which):
        return units[phase].at[pl.ds(pl.multiple_of(which * UNIT, TILE), UNIT), :]

    def unit_copy(phase, to_plane):
        return pltpu.make_async_remote_copy(
            src_ref=unit_lines(phase, plane),
            dst_ref=unit_lines(phase, plane),
            send_sem=unit_send.at[phase, to_plane],
            recv_sem=unit_recv.at[phase, plane],
            device_id={"date": to_plane * BAND + spot},
        )

    def unit_arrival(phase, source):
        return pltpu.make_async_remote_copy(
            src_ref=unit_lines(phase, source),
            dst_ref=unit_lines(phase, source),
            send_sem=unit_send.at[phase, source],
            recv_sem=unit_recv.at[phase, source],
            device_id={"date": source * BAND + spot},
        )

    def other_plane(turn):
        return lax.rem(plane + turn, planes)

    def unit_start(phase):
        units[phase][pl.ds(pl.multiple_of(plane * UNIT, TILE), UNIT), :] = sums[phase, :UNIT] * scale[:UNIT]

        @pl.loop(1, planes)
        def _(turn):
            unit_copy(phase, other_plane(turn)).start()

    def ratio_of(near, far_side, first_power, second_power):
        squares = [v * v for v in (near, far_side)]
        squares = [v + pltpu.roll(v, CAP, 0) for v in squares]
        level = jnp.sqrt(jnp.where(own_rows, squares[0], squares[1]))
        return level / jnp.sqrt((first_power + EPSILON) * (second_power + EPSILON))

    def parcel(to):
        return pl.ds(pl.multiple_of(to * 3 * TILE, TILE), 3 * TILE)

    def slot_copy(phase, to):
        return pltpu.make_async_remote_copy(
            src_ref=outboxes[phase].at[parcel(to), :],
            dst_ref=plane_inbox.at[phase, spot],
            send_sem=slot_send.at[phase, to],
            recv_sem=slot_recv.at[phase, spot],
            device_id={"date": plane * BAND + to},
        )

    def slot_arrival(phase, source):
        return pltpu.make_async_remote_copy(
            src_ref=outboxes[phase].at[parcel(source), :],
            dst_ref=plane_inbox.at[phase, source],
            send_sem=slot_send.at[phase, source],
            recv_sem=slot_recv.at[phase, source],
            device_id={"date": plane * BAND + source},
        )

    def choose(phase):
        unit = units[phase]
        for which in range(BAND):
            for at in range(CAP):
                for part in range(PARTS):
                    line = jnp.clip(index[which * CAP + at, part], 0, planes * UNIT)
                    row = (which * 4 + part // 2) * TILE + part % 2 * CAP + at
                    staged[phase, row:row + 1, :] = unit[pl.ds(line, 1), :]
        for which in range(BAND):
            near, far_side, first_power, second_power = (
                staged[phase, (which * 4 + at) * TILE:(which * 4 + at + 1) * TILE, :] for at in range(4)
            )
            ratio = ratio_of(near, far_side, first_power, second_power)
            outboxes[phase][which * 3 * TILE:(which + 1) * 3 * TILE, :] = jnp.concatenate(
                [near, far_side, ratio], axis=0
            )
        for step in (2, 3, 1):
            slot_copy(phase, spot ^ step).start()
        plane_inbox[phase, spot] = outboxes[phase][parcel(spot), :]

    index_copy.wait()

    last = len(chunks) - 1
    computed = 0
    for chunk in range(len(chunks) + LAG):
        if chunk <= last:
            forward(chunk)
        if chunk == 0:
            height_pass()
        while computed <= min(chunk - LAG, last):
            if computed == 0:
                @pl.loop(0, planes)
                def _(source):
                    @pl.when(jnp.logical_not(height_onward(source, 0) | height_onward(source, 1)))
                    def _():
                        height_arrival(source).wait_recv()

            compute(computed)
            start, width = chunks[computed]
            if (start + width) % steps == 0 and computed < last:
                unit_start(start // steps)
            computed += 1

    size = len(places) * CAP
    for at, piece in enumerate(split(sums[early] * scale, PIECES)):
        stack[at * LINES:(at + 1) * LINES, :] = piece
    chosen[...] = jnp.dot(picks[...], stack[...], preferred_element_type=jnp.float32)

    def peer(step):
        return lax.rem(me + step, devices)

    def out_copy(to):
        return pltpu.make_async_remote_copy(
            src_ref=outbox.at[to],
            dst_ref=inbox.at[me],
            send_sem=out_send.at[to],
            recv_sem=out_recv.at[me],
            device_id={"date": to},
        )

    def out_arrival(source):
        return pltpu.make_async_remote_copy(
            src_ref=outbox.at[source],
            dst_ref=inbox.at[source],
            send_sem=out_send.at[source],
            recv_sem=out_recv.at[source],
            device_id={"date": source},
        )

    @pl.loop(0, devices // BAND)
    def _(some):
        for one in range(BAND):
            which = lax.rem(plane + some, planes) * BAND + one
            near, far_side, first_power, second_power = (
                chosen[pl.ds(pl.multiple_of(which * size + at * TILE, TILE), TILE), :] for at in range(4)
            )
            for at, value in enumerate((near, far_side, ratio_of(near, far_side, first_power, second_power))):
                outbox[which, at] = value

        for one in range(BAND):
            to = lax.rem(plane + some, planes) * BAND + one

            @pl.when(to != me)
            def _():
                out_copy(to).start()


    inbox[me] = outbox[me]

    for phase in range(early):
        @pl.loop(1, planes)
        def _(turn):
            unit_arrival(phase, other_plane(turn)).wait_recv()

        choose(phase)

    @pl.loop(0, planes)
    def _(to_plane):
        @pl.when(height_direct(to_plane))
        def _():
            height_copy(to_plane).wait_send()

    @pl.loop(0, planes)
    def _(source):
        for up in range(2):
            @pl.when(height_onward(source, up))
            def _():
                height_relay(source, up).wait_send()

    for chunk in range(len(chunks)):
        for upper in range(2):
            plane_all(upper, chunk).wait_send()

            @pl.when(relays[upper])
            def _():
                relay_all(upper, chunk).wait_send()

    for phase in range(early):
        for step in range(1, BAND):
            slot_arrival(phase, spot ^ step).wait_recv()

    @pl.loop(1, devices)
    def _(step):
        out_arrival(peer(step)).wait_recv()

    for phase in range(early):
        @pl.loop(1, planes)
        def _(turn):
            unit_copy(phase, other_plane(turn)).wait_send()

        for step in range(1, BAND):
            slot_copy(phase, spot ^ step).wait_send()

    @pl.loop(1, devices)
    def _(step):
        out_copy(peer(step)).wait_send()


def assemble(planes, phases, inbox, plane_inbox, looks_out, coherence_out):
    tiles = phases // HALVES
    early = phases - 1
    part_lanes = LANES // HALVES
    look_rows = TILE // LOOK_ROWS
    looks = coherence_out.shape[0] // CAP
    left = lax.broadcasted_iota(jnp.int32, (TILE, LANES), 1) < part_lanes
    for quarter in range(BAND):
        for tile in range(tiles):
            for part in range(3):
                sides = []
                for half in range(HALVES):
                    phase = tile * HALVES + half
                    if phase < early:
                        sides.append(plane_inbox[phase, quarter, part * TILE:(part + 1) * TILE, :])
                    else:
                        value = inbox[quarter, part]
                        for other in range(1, planes):
                            value = value + inbox[other * BAND + quarter, part]
                        sides.append(value)
                here, there = sides
                values = (
                    jnp.where(left, here, pltpu.roll(there, part_lanes, 1)),
                    jnp.where(left, pltpu.roll(here, part_lanes, 1), there),
                )
                for look_row, value in enumerate(values):
                    for c in range(2):
                        upper = 1 - part if part < 2 else 1 - c
                        at = tile_of(tiles, quarter, upper, tile) * look_rows + look_row
                        piece = value[c * CAP:(c + 1) * CAP]
                        if part < 2:
                            looks_out[pl.ds(c * looks + at, CAP, stride=2 * looks), :] = piece
                        else:
                            coherence_out[pl.ds(at, CAP, stride=looks), :] = piece


def body(images, height_phase, baseline, pair_list, pair_owner):
    devices = lax.axis_size("date")
    rows, columns = images.shape[2:]
    lanes = columns // LOOK_COLS
    looks = rows // LOOK_ROWS
    planes = devices // BAND
    tiles = rows // (2 * BAND * TILE)
    phases = tiles * HALVES
    early = phases - 1
    blocks = columns // (HALVES * LANES)
    chunks = len(chunk_list(phases, blocks))
    dates = 2 * BAND
    pairs = pair_list.shape[0]
    assert lanes == LANES and rows == LOOK_ROWS * devices and TILE == 2 * LOOK_ROWS and HALVES == 2
    assert rows % (2 * BAND * TILE) == 0 and columns % (HALVES * LANES) == 0 and blocks > 5
    assert PIECES * LINES <= DEPTH
    vmem = pl.BlockSpec(memory_space=pltpu.VMEM)
    hbm = pl.BlockSpec(memory_space=pltpu.HBM)
    dma = pltpu.SemaphoreType.DMA
    tiled = images[0].reshape(2, rows // TILE, TILE, columns // LANES, LANES).transpose(0, 1, 3, 2, 4)
    inputs = [
        pltpu.with_memory_space_constraint(v, pltpu.HBM)
        for v in (tiled, height_phase, baseline[None], pair_list.T, pair_owner.T)
    ]
    scratch = [
        pltpu.VMEM((2, 2, phases * blocks, dates * TILE, LANES), jnp.float32),
        pltpu.VMEM((planes, LOOK_ROWS, columns), jnp.float32),
        pltpu.VMEM((2 * columns // HALVES, lanes), jnp.bfloat16),
        pltpu.VMEM((phases, LINES, lanes), jnp.float32),
        pltpu.VMEM((devices * TILE * CAP, DEPTH), jnp.bfloat16),
        pltpu.VMEM((DEPTH, lanes), jnp.bfloat16),
        pltpu.VMEM((devices * TILE * CAP, lanes), jnp.float32),
        pltpu.VMEM((devices, 3, TILE, lanes), jnp.float32),
        pltpu.VMEM((1, devices), jnp.float32),
        pltpu.VMEM((2, pairs), jnp.int32),
        pltpu.VMEM((1, pairs), jnp.int32),
        pltpu.VMEM((BAND * CAP, LANES), jnp.int32),
        pltpu.SMEM((BAND * CAP, LANES), jnp.int32),
        pltpu.VMEM((early, BAND * 4 * TILE, lanes), jnp.float32),
    ]
    scratch += [pltpu.VMEM((planes * UNIT + TILE, lanes), jnp.float32)] * early
    scratch += [pltpu.VMEM((BAND * 3 * TILE, lanes), jnp.float32)] * early
    size = sum(math.prod(s.shape) * jnp.dtype(s.dtype).itemsize for s in scratch)
    scratch += [
        pltpu.SemaphoreType.REGULAR((planes - 1,)),
        dma((4,)),
        dma((2, chunks)),
        dma((2, chunks)),
        dma((2, chunks, BAND)),
        dma((2, chunks)),
        dma((planes,)),
        dma((planes,)),
        dma((2, planes)),
        dma((early, planes)),
        dma((early, planes)),
        dma((early, BAND)),
        dma((early, BAND)),
        dma((devices,)),
        dma((devices,)),
    ]
    arrived = pl.pallas_call(
        functools.partial(kernel, devices, phases),
        out_shape=(
            jax.ShapeDtypeStruct((devices, 3, TILE, lanes), jnp.float32),
            jax.ShapeDtypeStruct((early, BAND, 3 * TILE, lanes), jnp.float32),
        ),
        in_specs=[hbm] * 5,
        out_specs=(vmem, vmem),
        scratch_shapes=scratch,
        compiler_params=pltpu.CompilerParams(
            collective_id=0, has_side_effects=True, vmem_limit_bytes=size + (6 << 20)
        ),
    )(*inputs)
    look, coherence = pl.pallas_call(
        functools.partial(assemble, planes, phases),
        out_shape=(
            jax.ShapeDtypeStruct((CAP * 2 * looks, lanes), jnp.float32),
            jax.ShapeDtypeStruct((CAP * looks, lanes), jnp.float32),
        ),
        in_specs=[vmem, vmem],
        out_specs=(vmem, vmem),
        compiler_params=pltpu.CompilerParams(vmem_limit_bytes=8 << 20),
    )(*arrived)
    return look.reshape(CAP, 2, looks, lanes), coherence.reshape(CAP, looks, lanes)


def solution(mesh):
    in_specs = (
        P(("groups", "date"), None, None, None),
        P(("groups", "date"), None),
        P("groups"),
        P(),
        P(),
    )
    out_specs = (P(("groups", "date"), None, None, None), P(("groups", "date"), None, None))
    return jax.shard_map(body, mesh=mesh, in_specs=in_specs, out_specs=out_specs, check_vma=False)
```
